32 devices in a mesh: dp: 4 (over z), ctx: 8 (over y, x, core).
Axes of the slice: x: 2, y: 2, z: 4, core: 2. Of those that a mesh axis runs over, the one named last changes fastest.
Arguments:
- inputs: bfloat16 [4, 1024, 4096], P('dp', 'ctx'), may hold values from -6 to 6
- queries: bfloat16 [4, 1024, 4096], P('dp', 'ctx'), may hold values from -384 to 384
- keys_values: bfloat16 [4, 1024, 2, 512], P('dp', 'ctx'), may hold values from -6 to 6
- out_grad: bfloat16 [4, 1024, 4096], P('dp', 'ctx'), may hold values from -6 to 6
- tree_mask: int32 [4, 8, 8], P('dp', 'ctx'), may hold values from 0 to 1, as said below
Outputs:
- attn_out: bfloat16 [4, 1024, 4096], P('dp', 'ctx')
- query_grad: bfloat16 [4, 1024, 4096], P('dp', 'ctx')
- key_weight_grad: float32 [4096, 512], P(('dp', 'ctx'))
- value_weight_grad: float32 [4096, 512], P(('dp', 'ctx'))
The draws below stay inside these ranges and needn't reach their ends.
Inputs may be any that keep to these rules, and one draw needn't show every extreme that they name: tree_mask[s,a,b] is 1 exactly where block b is block a or an ancestor of block a in the same tree of sequence s; a tree's blocks are consecutive, its first block is its root, every ancestor comes before its descendants, and blocks 0 and 1 belong to one tree.
All inputs are finite; a program needn't handle non-finite values.
Results may differ from the reference program's by a relative error of at most 0.029.
Values may be sent and summed in bfloat16 or wider, within the bound.
No kernel may reach another device: no remote copies, remote signals or barrier semaphores. Data moves between devices by JAX's collectives and lax.ppermute only.
A program may use at most 128 MiB of HBM per device.

```python
import math
import jax
import jax.numpy as jnp
from jax import lax

D = 4096
HEADS = 32
KV_HEADS = 4
HEAD_DIM = 128
BLOCK = 128
NBLK = 8
SEQ_LEN = 1024
SEQS = 4


def draw_queries(key, part):
    normal_part = jnp.clip(jax.random.normal(key, (SEQS, SEQ_LEN, HEADS, HEAD_DIM), jnp.float32), -6.0, 6.0)
    return normal_part.reshape(SEQS, SEQ_LEN, HEADS * HEAD_DIM).astype(jnp.bfloat16)


def one_tree_set(key):
    first_key, second_key, third_key = jax.random.split(key, 3)
    indices = jnp.arange(NBLK, dtype=jnp.int32)
    starts = (jax.random.randint(first_key, (NBLK,), 0, 12) == 0) & (indices != 1) | (indices == 0)
    tree_first = lax.cummax(jnp.where(starts, indices, 0), axis=0)
    chained = jax.random.randint(second_key, (NBLK,), 0, 2) == 0
    spans = jnp.maximum(indices - tree_first, 1)
    picked = tree_first + jax.random.randint(third_key, (NBLK,), 0, spans)
    parents = jnp.where(starts, indices, jnp.where(chained, indices - 1, picked))

    def fill_row(row_index, ancestors):
        inherited = jnp.where(starts[row_index], jnp.zeros((NBLK,), jnp.int32), ancestors[parents[row_index]])
        inherited = inherited.at[row_index].set(1)
        return ancestors.at[row_index].set(inherited)
    return lax.fori_loop(0, NBLK, fill_row, jnp.zeros((NBLK, NBLK), jnp.int32))


def draw_tree_mask(key, part):
    seq_keys = jax.random.split(jax.random.fold_in(key, 5), SEQS)
    return jax.vmap(one_tree_set)(seq_keys)


def with_spikes(drawn, own_key, source, target, blocks, factor):
    def block_of(dim):
        return (jnp.arange(drawn.shape[dim]) // (drawn.shape[dim] // blocks)).reshape((-1,) + (1,) * (drawn.ndim - 1 - dim))

    first = jax.random.permutation(own_key, blocks)[block_of(target)]
    other_side = (block_of(target) + blocks // 2) % blocks
    return jnp.where((block_of(source) == first) | (block_of(source) == other_side), factor * drawn, drawn)


def level_of(rng, extent, cuts, least, high):
    def one(dim, blocks):
        heights = jax.random.uniform(jax.random.fold_in(jax.random.fold_in(rng, 6), dim), (blocks,), jnp.float32, least / len(cuts), high / len(cuts))
        return jnp.repeat(jnp.exp(heights), extent[dim] // blocks).reshape((-1,) + (1,) * (len(extent) - dim - 1))

    level = one(*cuts[0])
    for cut in cuts[1:]:
        level = level * one(*cut)
    return level


def centred(own_key, dims, deviation, reach, cuts=(), kind=jnp.bfloat16):
    gain = level_of(own_key, dims, cuts, -0.22, 0.18) if cuts else 1.0
    values = jax.random.normal(own_key, dims, jnp.float32) * deviation * gain
    return jnp.minimum(jnp.maximum(values, -reach), reach).astype(kind)


def heavy_noise(rng, dims, scale, most, pieces, heavy, kind=jnp.bfloat16):
    array = scale * jax.random.normal(rng, dims, jnp.float32)
    if pieces:
        array = array * level_of(rng, dims, pieces, -0.22, 0.18)
    return jnp.clip(with_spikes(array, jax.random.fold_in(rng, 3), *heavy), -most, most).astype(kind)


def setup_inputs(seed: int = 0) -> dict:
    seeds = jax.random.split(jax.random.key(seed), 6)
    return {
        "inputs": heavy_noise(seeds[0], (SEQS, SEQ_LEN, D), 1.0, 6.0, ((0, 4), (1, 8)), (1, 2, 8, 2.0)),
        "queries": draw_queries(jax.random.fold_in(seeds[5], 71), 0),
        "keys_values": centred(seeds[2], (SEQS, SEQ_LEN, 2, KV_HEADS * HEAD_DIM), 1.0, 6.0, ((0, 4), (1, 8))),
        "out_grad": centred(seeds[3], (SEQS, SEQ_LEN, HEADS * HEAD_DIM), 1.0, 6.0, ((0, 4), (1, 8))),
        "tree_mask": draw_tree_mask(jax.random.fold_in(seeds[5], 71), 0),
    }


def allowed_tokens(block_rows):
    expanded = jnp.repeat(jnp.repeat(block_rows, BLOCK, axis=0), BLOCK, axis=1) == 1
    positions = jnp.arange(SEQ_LEN)
    query_pos = positions[:, None]
    key_pos = positions[None, :]
    same_block = query_pos // BLOCK == key_pos // BLOCK
    return expanded & (jnp.logical_not(same_block) | (key_pos <= query_pos))

def one_sequence(queries_s, kv_s, grad_s, mask_s):
    allowed = allowed_tokens(mask_s)
    ratio = HEADS // KV_HEADS
    score_scale = 1.0 / math.sqrt(HEAD_DIM)
    key_heads = kv_s[:, 0].reshape(SEQ_LEN, KV_HEADS, HEAD_DIM)
    value_heads = kv_s[:, 1].reshape(SEQ_LEN, KV_HEADS, HEAD_DIM)
    query_heads = queries_s.reshape(SEQ_LEN, HEADS, HEAD_DIM)
    grad_heads = grad_s.reshape(SEQ_LEN, HEADS, HEAD_DIM)

    def one_head(head_index):
        group = head_index // ratio
        query_one = lax.dynamic_index_in_dim(query_heads, head_index, 1, keepdims=False)
        grad_one = lax.dynamic_index_in_dim(grad_heads, head_index, 1, keepdims=False)
        key_one = lax.dynamic_index_in_dim(key_heads, group, 1, keepdims=False)
        value_one = lax.dynamic_index_in_dim(value_heads, group, 1, keepdims=False)
        scores = jnp.dot(query_one, key_one.T, preferred_element_type=jnp.float32) * score_scale
        row_max = lax.optimization_barrier(jnp.max(jnp.where(allowed, scores, -jnp.inf), axis=1, keepdims=True))
        row_sum = lax.optimization_barrier(jnp.sum(jnp.where(allowed, jnp.exp(scores - row_max), 0.0), axis=1, keepdims=True))
        log_total = row_max + jnp.log(row_sum)
        weights = jnp.where(allowed, jnp.exp(scores - log_total), 0.0)
        probs_low = weights.astype(jnp.bfloat16)
        attn_one = jnp.dot(probs_low, value_one, preferred_element_type=jnp.float32).astype(jnp.bfloat16)
        delta = lax.optimization_barrier(jnp.sum(grad_one.astype(jnp.float32) * attn_one.astype(jnp.float32), axis=1, keepdims=True))
        prob_grad = jnp.dot(grad_one, value_one.T, preferred_element_type=jnp.float32)
        score_grad = (probs_low.astype(jnp.float32) * (prob_grad - delta)).astype(jnp.bfloat16)
        query_part = jnp.dot(score_grad, key_one, preferred_element_type=jnp.float32) * score_scale
        key_part = jnp.dot(score_grad.T, query_one, preferred_element_type=jnp.float32) * score_scale
        value_part = jnp.dot(probs_low.T, grad_one, preferred_element_type=jnp.float32)
        return (attn_one, query_part.astype(jnp.bfloat16), key_part, value_part)
    attn_all, query_all, key_all, value_all = lax.map(one_head, jnp.arange(HEADS))
    attn_seq = jnp.transpose(attn_all, (1, 0, 2)).reshape(SEQ_LEN, HEADS * HEAD_DIM)
    query_seq = jnp.transpose(query_all, (1, 0, 2)).reshape(SEQ_LEN, HEADS * HEAD_DIM)
    key_sum = key_all.reshape(KV_HEADS, ratio, SEQ_LEN, HEAD_DIM).sum(axis=1)
    value_sum = value_all.reshape(KV_HEADS, ratio, SEQ_LEN, HEAD_DIM).sum(axis=1)
    key_grad = jnp.transpose(key_sum, (1, 0, 2)).reshape(SEQ_LEN, KV_HEADS * HEAD_DIM).astype(jnp.bfloat16)
    value_grad = jnp.transpose(value_sum, (1, 0, 2)).reshape(SEQ_LEN, KV_HEADS * HEAD_DIM).astype(jnp.bfloat16)
    return (attn_seq, query_seq, jnp.concatenate([key_grad, value_grad], axis=1))

def reference(inputs, queries, keys_values, out_grad, tree_mask):
    kv_width = KV_HEADS * HEAD_DIM
    attn_list = []
    query_list = []
    weight_sum = jnp.zeros((D, 2 * kv_width), jnp.float32)
    for sequence in range(SEQS):
        attn_seq, query_seq, both_grads = one_sequence(queries[sequence], keys_values[sequence], out_grad[sequence], tree_mask[sequence])
        attn_list.append(attn_seq)
        query_list.append(query_seq)
        weight_sum = weight_sum + jnp.dot(inputs[sequence].T, both_grads, preferred_element_type=jnp.float32)
    grad_scale = 1.0 / math.sqrt(SEQS * SEQ_LEN)
    weight_sum = weight_sum * grad_scale
    return (jnp.stack(attn_list), jnp.stack(query_list), weight_sum[:, :kv_width], weight_sum[:, kv_width:])
```

```python
import functools
import math

import jax
import jax.numpy as jnp
from jax import lax
from jax.experimental import pallas as pl
from jax.experimental.pallas import tpu as pltpu
from jax.sharding import PartitionSpec as P

HEADS = 32
KV_HEADS = 4
HEAD_DIM = 128
BLOCK = 128
RATIO = HEADS // KV_HEADS
NEG = -1e30
NT = (((1,), (1,)), ((), ()))


def swap(value, axis, mask):
    pairs = [(i, i ^ mask) for i in range(lax.axis_size(axis))]
    return lax.ppermute(value, axis, pairs)


def dot(a, b, dims=(((1,), (0,)), ((), ()))):
    return lax.dot_general(a, b, dims, preferred_element_type=jnp.float32)


def attention_kernel(pieces, blocks_here, steps, per_step, where_ref, own_mask, peer_mask, *refs):
    own_q, peer_q, own_g, peer_g = refs[:4]
    kv_refs = refs[4 : 4 + pieces]
    own_o, peer_o, own_dq, peer_dq = refs[4 + pieces : 8 + pieces]
    grad_refs = refs[8 + pieces : 8 + 2 * pieces]
    bias, keys, values, keys_t, values_t, key_acc, value_acc = refs[8 + 2 * pieces :]
    group, step = pl.program_id(0), pl.program_id(1)
    rows = 2 * blocks_here * BLOCK
    score_scale = 1.0 / math.sqrt(HEAD_DIM)
    exp_scale = score_scale * math.log2(math.e)

    @pl.when((group == 0) & (step == 0))
    def _():
        me = where_ref[0]
        key_pos = lax.broadcasted_iota(jnp.int32, (BLOCK, BLOCK), 0)
        query_pos = lax.broadcasted_iota(jnp.int32, (BLOCK, BLOCK), 1)
        causal = jnp.where(key_pos <= query_pos, 0.0, NEG)
        for piece in range(pieces):
            for s in range(2 * blocks_here):
                key_device = jnp.bitwise_xor(me, 2 * piece + s // blocks_here)
                key_block = key_device * blocks_here + s % blocks_here
                for t in range(2 * blocks_here):
                    query_device = jnp.bitwise_xor(me, t // blocks_here)
                    query_block = query_device * blocks_here + t % blocks_here
                    mask_ref = own_mask if t < blocks_here else peer_mask
                    other = jnp.where(mask_ref[t % blocks_here, key_block] == 1, 0.0, NEG)
                    same = key_block == query_block
                    tile = jnp.where(same, causal, other)
                    bias[
                        piece * rows + s * BLOCK : piece * rows + (s + 1) * BLOCK,
                        t * BLOCK : (t + 1) * BLOCK,
                    ] = tile

    @pl.when(step == 0)
    def _():
        for piece in range(pieces):
            part = slice(piece * rows, (piece + 1) * rows)
            key_part = kv_refs[piece][:, :HEAD_DIM]
            value_part = kv_refs[piece][:, HEAD_DIM:]
            keys[part, :] = key_part
            values[part, :] = value_part
            keys_t[:, part] = key_part.T
            values_t[:, part] = value_part.T
        key_acc[...] = jnp.zeros_like(key_acc)
        value_acc[...] = jnp.zeros_like(value_acc)

    half = rows // 2
    for i in range(per_step):
        columns = slice(i * HEAD_DIM, (i + 1) * HEAD_DIM)
        query = jnp.concatenate([own_q[0, :, columns], peer_q[:, columns]], axis=0)
        grad = jnp.concatenate([own_g[0, :, columns], peer_g[:, columns]], axis=0)
        scores = dot(keys[...], query, NT) + bias[...]
        top = jnp.max(scores, axis=0, keepdims=True) * exp_scale
        weights = jnp.exp2(scores * exp_scale - top)
        total = jnp.sum(weights, axis=0, keepdims=True)
        probs = weights * (1.0 / total)
        probs_low = probs.astype(jnp.bfloat16)
        prob_grad = dot(values[...], grad, NT)
        delta = jnp.sum(probs * prob_grad, axis=0, keepdims=True)
        score_grad = (probs * (prob_grad - delta)).astype(jnp.bfloat16)
        value_acc[...] += dot(probs_low, grad)
        key_acc[...] += dot(score_grad, query)
        out = dot(values_t[...], probs_low).T.astype(jnp.bfloat16)
        query_grad = (dot(keys_t[...], score_grad) * score_scale).T.astype(jnp.bfloat16)
        own_o[:, columns] = out[:half]
        peer_o[:, columns] = out[half:]
        own_dq[:, columns] = query_grad[:half]
        peer_dq[:, columns] = query_grad[half:]

    @pl.when(step == steps - 1)
    def _():
        for piece in range(pieces):
            part = slice(piece * rows, (piece + 1) * rows)
            grad_refs[piece][:, :HEAD_DIM] = (key_acc[part, :] * score_scale).astype(jnp.bfloat16)
            grad_refs[piece][:, HEAD_DIM:] = value_acc[part, :].astype(jnp.bfloat16)


def attention(me, core, own_mask, peer_mask, queries, peer_q, out_grad, peer_g, kv_pieces, first):
    tokens = queries.shape[1]
    blocks_here = tokens // BLOCK
    rows = 2 * tokens
    pieces = len(kv_pieces)
    groups = kv_pieces[0].shape[1] // (2 * HEAD_DIM)
    per_step = 2
    steps = RATIO // per_step
    wide = per_step * HEAD_DIM
    half_steps = KV_HEADS // 2 * steps
    where = jnp.stack([me, core]).astype(jnp.int32)

    def own_in(g, h, where_ref, *_):
        return (0, 0, where_ref[1] * half_steps + (first + g) * steps + h)

    def peer_in(g, h, *_):
        return (0, (first + g) * steps + h)

    def out_map(g, h, *_):
        return (0, g * steps + h)

    def group_map(g, h, *_):
        return (0, g)

    keys_all = pieces * rows
    out_cols = groups * RATIO * HEAD_DIM
    result = pl.pallas_call(
        functools.partial(attention_kernel, pieces, blocks_here, steps, per_step),
        grid_spec=pltpu.PrefetchScalarGridSpec(
            num_scalar_prefetch=3,
            grid=(groups, steps),
            in_specs=[
                pl.BlockSpec((1, tokens, wide), own_in),
                pl.BlockSpec((tokens, wide), peer_in),
                pl.BlockSpec((1, tokens, wide), own_in),
                pl.BlockSpec((tokens, wide), peer_in),
            ]
            + [pl.BlockSpec((rows, 2 * HEAD_DIM), group_map)] * pieces,
            out_specs=[pl.BlockSpec((tokens, wide), out_map)] * 4
            + [pl.BlockSpec((rows, 2 * HEAD_DIM), group_map)] * pieces,
            scratch_shapes=[
                pltpu.VMEM((keys_all, rows), jnp.float32),
                pltpu.VMEM((keys_all, HEAD_DIM), jnp.bfloat16),
                pltpu.VMEM((keys_all, HEAD_DIM), jnp.bfloat16),
                pltpu.VMEM((HEAD_DIM, keys_all), jnp.bfloat16),
                pltpu.VMEM((HEAD_DIM, keys_all), jnp.bfloat16),
                pltpu.VMEM((keys_all, HEAD_DIM), jnp.float32),
                pltpu.VMEM((keys_all, HEAD_DIM), jnp.float32),
            ],
        ),
        out_shape=[jax.ShapeDtypeStruct((tokens, out_cols), jnp.bfloat16)] * 4
        + [jax.ShapeDtypeStruct((rows, 2 * HEAD_DIM * groups), jnp.bfloat16)] * pieces,
        compiler_params=pltpu.CompilerParams(vmem_limit_bytes=56 * 1024 * 1024),
        cost_estimate=pl.CostEstimate(
            flops=12 * groups * RATIO * rows * keys_all * HEAD_DIM,
            transcendentals=groups * RATIO * rows * keys_all,
            bytes_accessed=16 * tokens * out_cols,
        ),
        name="attention",
    )(where, own_mask, peer_mask, queries, peer_q, out_grad, peer_g, *kv_pieces)
    return result[:4], result[4:]


def body(inputs, queries, keys_values, out_grad, tree_mask):
    tokens = queries.shape[1]
    width = queries.shape[2]
    half = width // 2
    count = lax.axis_size("ctx")
    data_size = lax.axis_size("dp")
    me = lax.axis_index("ctx")
    data_me = lax.axis_index("dp")
    core = me % 2
    chip = me // 2
    chips = count // 2
    hops = [2 * p for p in range(1, chips)]

    own_mask = tree_mask[0]
    peer_mask = swap(own_mask, "ctx", 1)
    kv = keys_values[0].reshape(tokens, 2, KV_HEADS, HEAD_DIM)
    parts = [kv[:, :, g].reshape(tokens, 2 * HEAD_DIM) for g in range(KV_HEADS)]
    low = jnp.concatenate(parts[:2], axis=1)
    high = jnp.concatenate(parts[2:], axis=1)
    kv_keep = jnp.where(core == 0, low, high)
    kv_send = jnp.where(core == 0, high, low)
    kv_own = jnp.concatenate([kv_keep, swap(kv_send, "ctx", 1)], axis=0)
    peer_start = (1 - core) * half
    peer_q = swap(lax.dynamic_slice_in_dim(queries[0], peer_start, half, 1), "ctx", 1)
    peer_g = swap(lax.dynamic_slice_in_dim(out_grad[0], peer_start, half, 1), "ctx", 1)
    kv_pieces = [kv_own] + [swap(kv_own, "ctx", k) for k in hops]

    slices = inputs[0].reshape(tokens, data_size, chips, width // (data_size * chips))
    rows_out = width // (data_size * count)

    def slice_for(k):
        return lax.dynamic_index_in_dim(slices, (me ^ k) // 2, 2, keepdims=False)

    in_own = jnp.stack([slice_for(0)] + [swap(slice_for(k), "ctx", k) for k in hops])
    in_peer = swap(in_own, "ctx", 1)
    in_all = jnp.concatenate([in_own, in_peer], axis=1).reshape(chips * 2 * tokens, width // chips)

    (own_o, peer_o, own_dq, peer_dq), grads = attention(
        me, core, own_mask, peer_mask, queries, peer_q, out_grad, peer_g, kv_pieces, 0
    )

    def join(mine, other):
        got = swap(other, "ctx", 1)
        whole = jnp.where(
            core == 0, jnp.concatenate([mine, got], 1), jnp.concatenate([got, mine], 1)
        )
        return whole[None]

    attn_out = join(own_o, peer_o)
    query_grad = join(own_dq, peer_dq)

    total = grads[0].astype(jnp.float32)
    for p, k in enumerate(hops):
        total = total + swap(grads[p + 1], "ctx", k).astype(jnp.float32)
    total = total.astype(jnp.bfloat16)
    gathered = jnp.concatenate([total] + [swap(total, "ctx", k) for k in hops], axis=0)
    grad_scale = 1.0 / math.sqrt(tokens * count * data_size)
    product = dot(in_all, gathered, (((0,), (0,)), ((), ()))) * grad_scale
    product = product.reshape(data_size, 2 * rows_out, 4 * HEAD_DIM)

    def chunk(k):
        return lax.dynamic_index_in_dim(product, data_me ^ k, 0, keepdims=False)

    mine = chunk(0)
    for k in range(1, data_size):
        mine = mine + swap(chunk(k).astype(jnp.bfloat16), "dp", k).astype(jnp.float32)
    mine = mine.reshape(2, rows_out, 4 * HEAD_DIM)
    keep = lax.dynamic_index_in_dim(mine, core, 0, keepdims=False)
    got = swap(lax.dynamic_index_in_dim(mine, 1 - core, 0, keepdims=False), "ctx", 1)
    first = jnp.where(core == 0, keep, got).reshape(rows_out, 2, 2, HEAD_DIM)
    last = jnp.where(core == 0, got, keep).reshape(rows_out, 2, 2, HEAD_DIM)
    both = jnp.concatenate([first, last], axis=1)
    kv_width = KV_HEADS * HEAD_DIM
    return (
        attn_out,
        query_grad,
        both[:, :, 0].reshape(rows_out, kv_width),
        both[:, :, 1].reshape(rows_out, kv_width),
    )


def solution(mesh):
    in_specs = (
        P("dp", "ctx", None),
        P("dp", "ctx", None),
        P("dp", "ctx", None, None),
        P("dp", "ctx", None),
        P("dp", "ctx", None),
    )
    out_specs = (
        P("dp", "ctx", None),
        P("dp", "ctx", None),
        P(("dp", "ctx"), None),
        P(("dp", "ctx"), None),
    )
    return jax.shard_map(body, mesh=mesh, in_specs=in_specs, out_specs=out_specs, check_vma=False)
```

```python
import functools
import math

import jax
import jax.numpy as jnp
from jax import lax
from jax.experimental import pallas as pl
from jax.experimental.pallas import tpu as pltpu
from jax.sharding import PartitionSpec as P

HEADS = 32
KV_HEADS = 4
HEAD_DIM = 128
BLOCK = 128
RATIO = HEADS // KV_HEADS
NEG = -1e30
NT = (((1,), (1,)), ((), ()))


def swap(value, axis, mask):
    pairs = [(i, i ^ mask) for i in range(lax.axis_size(axis))]
    return lax.ppermute(value, axis, pairs)


def dot(a, b, dims=(((1,), (0,)), ((), ()))):
    return lax.dot_general(a, b, dims, preferred_element_type=jnp.float32)


def copy_columns(chips, span, wide, chip, inputs_ref, outs, start):
    for k, out in enumerate(outs):
        for i, d in enumerate(span):
            source = pl.ds(pl.multiple_of((d * chips + jnp.bitwise_xor(chip, k)) * wide, wide), wide)
            out[:, start + i * wide : start + (i + 1) * wide] = inputs_ref[0, :, source]


def attention_kernel(pieces, blocks_here, steps, per_step, span, wide, where_ref, own_mask, peer_mask, *refs):
    if span:
        inputs_ref, *refs = refs
    own_q, peer_q, own_g, peer_g = refs[:4]
    kv_refs = refs[4 : 4 + pieces]
    own_o, own_dq, peer_out = refs[4 + pieces : 7 + pieces]
    grad_refs = refs[7 + pieces : 7 + 2 * pieces]
    (mask_cols, causal, keys, values, keys_t, values_t, key_acc, value_acc, scores, weights, flows) = refs[
        7 + 2 * pieces :
    ]
    group, step = pl.program_id(0), pl.program_id(1)
    rows = 2 * blocks_here * BLOCK
    half = rows // 2
    blocks = 2 * blocks_here
    tiles = pieces * blocks
    score_scale = 1.0 / math.sqrt(HEAD_DIM)
    exp_scale = score_scale * math.log2(math.e)
    low = jnp.bfloat16

    @pl.when((group == 0) & (step == 0))
    def _():
        me = where_ref[0]
        lane = lax.broadcasted_iota(jnp.int32, (BLOCK, HEAD_DIM), 1)
        for t in range(blocks):
            mask_ref = own_mask if t < blocks_here else peer_mask
            tile = jnp.zeros((BLOCK, HEAD_DIM), jnp.float32)
            for block in range(tiles):
                key_device = jnp.bitwise_xor(me, block // blocks_here)
                seen = mask_ref[t % blocks_here, key_device * blocks_here + block % blocks_here]
                tile = jnp.where(lane == block, jnp.where(seen == 1, 0.0, NEG), tile)
            mask_cols[t * BLOCK : (t + 1) * BLOCK, :] = tile.astype(low)
        for block in range(tiles):
            part = slice(block * BLOCK, (block + 1) * BLOCK)
            keys[part, HEAD_DIM:] = jnp.where(lane == block, 1.0, 0.0).astype(low)
            values[part, HEAD_DIM:] = jnp.where(lane < 3, 1.0, 0.0).astype(low)
        key_pos = lax.broadcasted_iota(jnp.int32, (BLOCK, BLOCK), 0)
        query_pos = lax.broadcasted_iota(jnp.int32, (BLOCK, BLOCK), 1)
        causal[...] = jnp.where(key_pos <= query_pos, 0.0, NEG)

    @pl.when(step == 0)
    def _():
        for piece in range(2 * pieces):
            part = slice(piece * half, (piece + 1) * half)
            column = piece % 2 * 2 * HEAD_DIM
            key_part = kv_refs[piece // 2][:, column : column + HEAD_DIM]
            value_part = kv_refs[piece // 2][:, column + HEAD_DIM : column + 2 * HEAD_DIM]
            keys[part, :HEAD_DIM] = key_part
            values[part, :HEAD_DIM] = value_part
            keys_t[:, part] = key_part.T
            values_t[:, part] = value_part.T
        key_acc[...] = jnp.zeros_like(key_acc)
        value_acc[...] = jnp.zeros_like(value_acc)

    state = [dict() for _ in range(per_step)]

    def take(own, peer, i):
        columns = slice(i * HEAD_DIM, (i + 1) * HEAD_DIM)
        return jnp.concatenate([own[0, :, columns], peer[0, :, columns]], axis=0)

    def fold(x, op):
        return op(x.reshape(x.shape[0] // 8, 8, x.shape[1]), axis=0)

    def score(i):
        query = jnp.concatenate([take(own_q, peer_q, i), mask_cols[...]], axis=1)
        top = None
        for tile in range(tiles):
            part = slice(tile * BLOCK, (tile + 1) * BLOCK)
            got = dot(keys[part, :], query, NT)
            if tile < blocks:
                here = slice(tile * BLOCK, (tile + 1) * BLOCK)
                cut = got[:, here] + causal[...]
                got = jnp.concatenate(
                    [x for x in (got[:, : here.start], cut, got[:, here.stop :]) if x.shape[1]], axis=1
                )
            scores[i, part, :] = got
            best = fold(got, jnp.max)
            top = best if top is None else jnp.maximum(top, best)
        state[i]["top"] = jnp.max(top, axis=0, keepdims=True) * exp_scale

    def soften(i):
        top = state[i]["top"]
        total = None
        for tile in range(tiles):
            part = slice(tile * BLOCK, (tile + 1) * BLOCK)
            weight = jnp.exp2(scores[i, part, :] * exp_scale - top)
            weights[part, i * rows : (i + 1) * rows] = weight.astype(low)
            add = fold(weight, jnp.sum)
            total = add if total is None else total + add
        state[i]["inverse"] = 1.0 / jnp.sum(total, axis=0, keepdims=True)

    def attend(i):
        columns = slice(i * HEAD_DIM, (i + 1) * HEAD_DIM)
        inverse = state[i]["inverse"]
        grad_t = (take(own_g, peer_g, i).T.astype(jnp.float32) * inverse).astype(low)
        out_t = dot(values_t[...], weights[:, i * rows : (i + 1) * rows]) * inverse
        delta = -jnp.sum(out_t * grad_t.astype(jnp.float32), axis=0, keepdims=True)
        out = out_t.astype(low).T
        own_o[:, columns] = out[:half]
        peer_out[:, columns] = out[half:]
        first = delta.astype(low).astype(jnp.float32)
        second = (delta - first).astype(low).astype(jnp.float32)
        third = delta - first - second
        line = lax.broadcasted_iota(jnp.int32, (HEAD_DIM, rows), 0)
        extra = jnp.where(
            line == 0, first, jnp.where(line == 1, second, jnp.where(line == 2, third, 0.0))
        ).astype(low)
        state[i]["grad_t"] = grad_t
        state[i]["both_t"] = jnp.concatenate([grad_t, extra], axis=0)

    def flow(i):
        both_t = state[i]["both_t"]
        span = slice(i * rows, (i + 1) * rows)
        for tile in range(tiles):
            part = slice(tile * BLOCK, (tile + 1) * BLOCK)
            got = dot(values[part, :], both_t)
            flows[part, span] = (weights[part, span].astype(jnp.float32) * got).astype(low)

    def finish(i):
        columns = slice(i * HEAD_DIM, (i + 1) * HEAD_DIM)
        span = slice(i * rows, (i + 1) * rows)
        query_grad = (dot(keys_t[...], flows[:, span]) * score_scale).astype(low).T
        own_dq[:, columns] = query_grad[:half]
        start = (RATIO + i) * HEAD_DIM
        peer_out[:, start : start + HEAD_DIM] = query_grad[half:]

    stages = [score, soften, attend, flow, finish]
    for slot in range(per_step + len(stages) - 1):
        for lag, stage in reversed(list(enumerate(stages))):
            if 0 <= slot - lag < per_step:
                stage(slot - lag)
    queries = jnp.concatenate([take(own_q, peer_q, i) for i in range(per_step)], axis=0)
    grads_t = jnp.concatenate([state[i]["grad_t"] for i in range(per_step)], axis=1)
    value_acc[...] += dot(weights[...], grads_t, NT)
    key_acc[...] += dot(flows[...], queries)

    @pl.when(step == steps - 1)
    def _():
        for piece in range(2 * pieces):
            part = slice(piece * half, (piece + 1) * half)
            column = piece % 2 * 2 * HEAD_DIM
            out = grad_refs[piece // 2]
            out[:, column : column + HEAD_DIM] = (key_acc[part, :] * score_scale).astype(low)
            out[:, column + HEAD_DIM : column + 2 * HEAD_DIM] = value_acc[part, :].astype(low)
        if span:
            copy_columns(pieces, span, wide, where_ref[0] // 2, inputs_ref, grad_refs, 4 * HEAD_DIM)


def attention(me, core, own_mask, peer_mask, queries, peer_q, out_grad, peer_g, kv_pieces, group, inputs=None, span=()):
    tokens = queries.shape[1]
    blocks_here = tokens // BLOCK
    rows = 2 * tokens
    pieces = len(kv_pieces)
    per_step = RATIO
    steps = RATIO // per_step
    wide = per_step * HEAD_DIM
    where = jnp.stack([me, core]).astype(jnp.int32)

    def heads_in(g, h, where_ref, *_):
        return (0, 0, (where_ref[1] * (KV_HEADS // 2) + group) * steps + h)

    def fixed(g, h, *_):
        return (0, 0)

    wide_in = inputs.shape[2] // (lax.axis_size("dp") * pieces) if span else 0
    extra = [inputs] if span else []
    grad_cols = 4 * HEAD_DIM + wide_in * len(span)
    keys_all = pieces * rows
    out_cols = RATIO * HEAD_DIM
    result = pl.pallas_call(
        functools.partial(attention_kernel, pieces, blocks_here, steps, per_step, span, wide_in),
        grid_spec=pltpu.PrefetchScalarGridSpec(
            num_scalar_prefetch=3,
            grid=(1, steps),
            in_specs=[pl.BlockSpec(x.shape, lambda *_: (0, 0, 0)) for x in extra]
            + [pl.BlockSpec((1, tokens, wide), heads_in)] * 4
            + [pl.BlockSpec((tokens, 4 * HEAD_DIM), fixed)] * pieces,
            out_specs=[pl.BlockSpec((tokens, wide), fixed)] * 2
            + [pl.BlockSpec((tokens, 2 * wide), fixed)]
            + [pl.BlockSpec((tokens, grad_cols), fixed)] * pieces,
            scratch_shapes=[
                pltpu.VMEM((rows, HEAD_DIM), jnp.bfloat16),
                pltpu.VMEM((BLOCK, BLOCK), jnp.float32),
                pltpu.VMEM((keys_all, 2 * HEAD_DIM), jnp.bfloat16),
                pltpu.VMEM((keys_all, 2 * HEAD_DIM), jnp.bfloat16),
                pltpu.VMEM((HEAD_DIM, keys_all), jnp.bfloat16),
                pltpu.VMEM((HEAD_DIM, keys_all), jnp.bfloat16),
                pltpu.VMEM((keys_all, HEAD_DIM), jnp.float32),
                pltpu.VMEM((keys_all, HEAD_DIM), jnp.float32),
                pltpu.VMEM((per_step, keys_all, rows), jnp.float32),
                pltpu.VMEM((keys_all, per_step * rows), jnp.bfloat16),
                pltpu.VMEM((keys_all, per_step * rows), jnp.bfloat16),
            ],
        ),
        out_shape=[jax.ShapeDtypeStruct((tokens, out_cols), jnp.bfloat16)] * 2
        + [jax.ShapeDtypeStruct((tokens, 2 * out_cols), jnp.bfloat16)]
        + [jax.ShapeDtypeStruct((tokens, grad_cols), jnp.bfloat16)] * pieces,
        compiler_params=pltpu.CompilerParams(vmem_limit_bytes=56 * 1024 * 1024),
        cost_estimate=pl.CostEstimate(
            flops=(24 if span else 1) * RATIO * rows * keys_all * HEAD_DIM,
            transcendentals=RATIO * rows * keys_all,
            bytes_accessed=16 * tokens * out_cols,
        ),
        name="attention",
    )(where, own_mask, peer_mask, *extra, queries, peer_q, out_grad, peer_g, *kv_pieces)
    return list(result[:3]), list(result[3:])


def small_call(kernel, name, scalars, operands, out_shape, cost=2_000_000, scratch=(), streamed=False):
    whole = pl.BlockSpec(memory_space=pltpu.VMEM)
    return pl.pallas_call(
        kernel,
        grid=(1,) if streamed else (),
        in_specs=[pl.BlockSpec(memory_space=pltpu.SMEM)]
        + [pl.BlockSpec(x.shape, lambda i, n=x.ndim: (0,) * n) if streamed else whole for x in operands],
        out_specs=jax.tree.map(lambda _: whole, out_shape),
        out_shape=out_shape,
        scratch_shapes=scratch,
        compiler_params=pltpu.CompilerParams(vmem_limit_bytes=32 * 1024 * 1024),
        cost_estimate=pl.CostEstimate(flops=0, transcendentals=0, bytes_accessed=cost),
        name=name,
    )(scalars, *operands)


def turn_kernel(offset, scalar_ref, *refs):
    *parts, out = refs
    tokens = parts[0].shape[0]
    for i, part in enumerate(parts):
        out[:, i * tokens : (i + 1) * tokens] = part[:, offset:].T


def product_kernel(plan, scale, scalar_ref, own_low, own_high, peer_low, peer_high, *refs):
    *refs, whole = refs
    pieces = len(refs) - len(plan)
    grads, outs = refs[:pieces], refs[pieces:]
    own_grad = jnp.concatenate([g[:, : 2 * HEAD_DIM] for g in grads], axis=0)
    peer_grad = jnp.concatenate([g[:, 2 * HEAD_DIM :] for g in grads], axis=0)
    half = own_low.shape[0]
    for i, (own, peer) in enumerate(((own_low, peer_low), (own_high, peer_high))):
        got = dot(own[...], own_grad) + dot(peer[...], peer_grad)
        whole[i * half : i * half + own.shape[0], :] = got * scale
    for chunks, out in zip(plan, outs):
        size = out.shape[0] // len(chunks)
        for i, k in enumerate(chunks):
            start = pl.multiple_of(jnp.bitwise_xor(scalar_ref[0], k) * size, size)
            out[i * size : (i + 1) * size, :] = whole[pl.ds(start, size), :].astype(out.dtype)


def pack_kernel(span, scalar_ref, inputs_ref, front, *outs):
    wide = (outs[0].shape[1] - front.shape[1]) // len(span)
    copy_columns(len(outs), span, wide, scalar_ref[0], inputs_ref, outs, front.shape[1])
    for out in outs[1:]:
        out[:, : front.shape[1]] = front[...]


def columns_for(inputs, me, k, chips, span):
    tokens, width = inputs.shape[1:]
    wide = width // (lax.axis_size("dp") * chips)
    shaped = inputs[0].reshape(tokens, -1, chips, wide)[:, span[0] : span[-1] + 1]
    part = lax.dynamic_index_in_dim(shaped, (me // 2) ^ k, 2, keepdims=False)
    return part.reshape(tokens, wide * len(span))


def pack(inputs, front, me, chips, span):
    tokens = inputs.shape[1]
    wide = inputs.shape[2] // (lax.axis_size("dp") * chips)
    if wide % HEAD_DIM:
        return [
            jnp.concatenate([front, columns_for(inputs, me, k, chips, span)], axis=1)
            for k in range(chips)
        ]
    return small_call(
        functools.partial(pack_kernel, span),
        "pack",
        (me // 2).reshape(1).astype(jnp.int32),
        [inputs, front],
        [jax.ShapeDtypeStruct((tokens, front.shape[1] + wide * len(span)), jnp.bfloat16)] * chips,
        cost=1,
    )


def settle_kernel(starts, scalar_ref, *refs):
    *parts, keep, send = refs
    size = keep.shape[0]
    core = scalar_ref[0]
    count = len(parts) // 2
    for first, out in ((core * size, keep), ((1 - core) * size, send)):
        for j in range(2):
            total = None
            for ref, start in zip(parts[j * count : (j + 1) * count], starts):
                part = ref[pl.ds(pl.multiple_of(first + start, size), size), :].astype(jnp.float32)
                total = part if total is None else total + part
            out[:, j * 2 * HEAD_DIM : (j + 1) * 2 * HEAD_DIM] = total


def close_kernel(scalar_ref, keep, got, key_out, value_out):
    core = scalar_ref[0]
    for side, ref in ((core, keep), (1 - core, got)):
        for i in range(2):
            span = pl.ds(pl.multiple_of((2 * side + i) * HEAD_DIM, HEAD_DIM), HEAD_DIM)
            key_out[:, span] = ref[:, 2 * i * HEAD_DIM : (2 * i + 1) * HEAD_DIM]
            value_out[:, span] = ref[:, (2 * i + 1) * HEAD_DIM : (2 * i + 2) * HEAD_DIM]


def join_kernel(scalar_ref, own_o_a, own_o_b, own_dq_a, own_dq_b, got_a, got_b, out, query_grad, sem):
    core = scalar_ref[0]
    wide = own_o_a.shape[1]
    copies = []
    for j, (whole, own) in enumerate(((out, (own_o_a, own_o_b)), (query_grad, (own_dq_a, own_dq_b)))):
        for i in range(2):
            other = (got_a, got_b)[i].at[:, j * wide : (j + 1) * wide]
            for side, ref in ((core, own[i]), (1 - core, other)):
                span = pl.ds(pl.multiple_of((2 * side + i) * wide, wide), wide)
                copies.append(pltpu.make_async_copy(ref, whole.at[0, :, span], sem.at[len(copies)]))
    for copy in copies:
        copy.start()
    for copy in copies:
        copy.wait()


def join(core_scalar, parts, shape):
    return pl.pallas_call(
        join_kernel,
        in_specs=[pl.BlockSpec(memory_space=pltpu.SMEM)]
        + [pl.BlockSpec(memory_space=pl.ANY)] * len(parts),
        out_specs=[pl.BlockSpec(memory_space=pltpu.VMEM)] * 2,
        out_shape=[jax.ShapeDtypeStruct(shape, jnp.bfloat16)] * 2,
        scratch_shapes=[pltpu.SemaphoreType.DMA((8,))],
        cost_estimate=pl.CostEstimate(flops=0, transcendentals=0, bytes_accessed=4_000_000),
        name="join",
    )(core_scalar, *parts)


def hold(values, *others):
    return lax.optimization_barrier((values, others))[0]


def body(inputs, queries, keys_values, out_grad, tree_mask):
    tokens = queries.shape[1]
    width = queries.shape[2]
    count = lax.axis_size("ctx")
    data_size = lax.axis_size("dp")
    me = lax.axis_index("ctx")
    data_me = lax.axis_index("dp")
    core = me % 2
    chips = count // 2
    hops = [2 * p for p in range(1, chips)]
    low, high = jnp.bfloat16, jnp.float32
    core_scalar = core.reshape(1).astype(jnp.int32)
    data_scalar = data_me.reshape(1).astype(jnp.int32)

    halves = [[], []]
    for source in (keys_values, swap(keys_values, "ctx", 1)):
        for j in range(2):
            both = source[0, :, j].reshape(tokens, 2, 2 * HEAD_DIM)
            both = lax.dynamic_index_in_dim(both, core, 1, keepdims=False)
            halves[0].append(both[:, :HEAD_DIM])
            halves[1].append(both[:, HEAD_DIM:])
    own_a, own_b = (jnp.concatenate(half, axis=1) for half in halves)
    pieces_a = [own_a] + [swap(own_a, "ctx", k) for k in hops]
    own_mask, queries_later, out_grad_later = hold((tree_mask[0], queries, out_grad), own_a)
    peer_mask = swap(own_mask, "ctx", 1)
    peer_q = swap(queries_later, "ctx", 1)
    peer_g = swap(out_grad_later, "ctx", 1)
    middle = data_size // 2
    whole_lanes = width // (data_size * chips) % HEAD_DIM == 0
    low_span, high_span = range(middle), range(middle, data_size)
    packed_b = pack(inputs, hold(own_b, peer_mask), me, chips, low_span)
    sends = hold(packed_b[1:], peer_q, peer_g)
    pieces_b = [own_b] + [swap(x, "ctx", k) for x, k in zip(sends, hops)]

    heads = (me, core, own_mask, peer_mask, queries, peer_q, out_grad, peer_g)
    if whole_lanes:
        outs_a, packed_a = attention(*heads, pieces_a, 0, inputs, high_span)
    else:
        outs_a, packed_a = attention(*heads, pieces_a, 0)
        packed_a = [
            jnp.concatenate([x, columns_for(inputs, me, k, chips, high_span)], axis=1)
            for k, x in enumerate(packed_a)
        ]
    back_a = [swap(x, "ctx", k) for x, k in zip(packed_a[1:], hops)]
    got_a = swap(outs_a[2], "ctx", 1)
    pieces_b = hold(pieces_b, outs_a[2])

    def turn(parts, streamed):
        return small_call(
            functools.partial(turn_kernel, 4 * HEAD_DIM),
            "turn",
            core_scalar,
            parts,
            jax.ShapeDtypeStruct((parts[0].shape[1] - 4 * HEAD_DIM, chips * tokens), low),
            cost=1,
            streamed=streamed,
        )

    own_low = turn(list(packed_b[:1]) + list(pieces_b[1:]), True)
    peer_low = swap(own_low, "ctx", 1)
    outs_b, grads_b = attention(*heads, pieces_b, 1)
    grads_b, back_a, got_a, peer_low = lax.optimization_barrier((grads_b, back_a, got_a, peer_low))
    back_b = [swap(x, "ctx", k) for x, k in zip(grads_b[1:], hops)]
    own_high = turn(list(packed_a[:1]) + list(back_a), False)
    peer_high = swap(own_high, "ctx", 1)

    def owned(mine, back):
        total = mine.astype(high)
        for x in back:
            total = total + x.astype(high)
        return total.astype(low)

    def gathered(total):
        return [total] + [swap(total, "ctx", k) for k in hops]

    scale = 1.0 / math.sqrt(tokens * count * data_size)
    rows_out = width // (data_size * count)
    size = 2 * rows_out
    pairwise = data_size == 4
    plan = [[0], [2], [3, 1]] if pairwise else [[k] for k in range(data_size)]
    kinds = [high, high, low] if pairwise else [high] + [low] * (data_size - 1)

    def product(grads):
        return small_call(
            functools.partial(product_kernel, plan, scale),
            "product",
            data_scalar,
            [own_low, own_high, peer_low, peer_high] + grads,
            [
                jax.ShapeDtypeStruct((size * len(chunks), 2 * HEAD_DIM), kind)
                for chunks, kind in zip(plan, kinds)
            ],
            scratch=[pltpu.VMEM((size * data_size, 2 * HEAD_DIM), high)],
        )

    folded = 4 * HEAD_DIM
    all_a = gathered(owned(packed_a[0][:, :folded], [x[:, :folded] for x in back_a]))
    all_b = gathered(owned(grads_b[0], back_b))
    chunks_a = product(all_a)
    all_b = hold(all_b, chunks_a)
    chunks_b = product(all_b)
    if pairwise:
        near_a = swap(chunks_a[2], "dp", 1)
        cross_a = (chunks_a[1] + near_a[:size].astype(high)).astype(low)
        near_b = swap(hold(chunks_b[2], cross_a), "dp", 1)
        cross_b = (chunks_b[1] + near_b[:size].astype(high)).astype(low)
        arrived = [[near_a, swap(cross_a, "dp", 2)], [near_b, swap(cross_b, "dp", 2)]]
        starts = [0, size, 0]
    else:
        arrived = [[swap(x[k], "dp", k) for k in range(1, data_size)] for x in (chunks_a, chunks_b)]
        cross_b = chunks_b[0]
        starts = [0] * data_size
    got_b = swap(hold(outs_b[2], chunks_b), "ctx", 1)
    parts = [outs_a[0], outs_b[0], outs_a[1], outs_b[1], got_a, got_b]
    attn_out, query_grad = join(core_scalar, hold(parts, cross_b), queries.shape)
    arrived, attn_out, query_grad = lax.optimization_barrier((arrived, attn_out, query_grad))
    kept, sent = small_call(
        functools.partial(settle_kernel, starts),
        "settle",
        core_scalar,
        [chunks_a[0]] + arrived[0] + [chunks_b[0]] + arrived[1],
        [jax.ShapeDtypeStruct((rows_out, 4 * HEAD_DIM), high)] * 2,
    )
    key_out, value_out = small_call(
        close_kernel,
        "close",
        core_scalar,
        [kept, swap(sent, "ctx", 1)],
        [jax.ShapeDtypeStruct((rows_out, KV_HEADS * HEAD_DIM), high)] * 2,
    )
    return attn_out, query_grad, key_out, value_out


def solution(mesh):
    in_specs = (
        P("dp", "ctx", None),
        P("dp", "ctx", None),
        P("dp", "ctx", None, None),
        P("dp", "ctx", None),
        P("dp", "ctx", None),
    )
    out_specs = (
        P("dp", "ctx", None),
        P("dp", "ctx", None),
        P(("dp", "ctx"), None),
        P(("dp", "ctx"), None),
    )
    return jax.shard_map(body, mesh=mesh, in_specs=in_specs, out_specs=out_specs, check_vma=False)
```

```python
import functools
import math

import jax
import jax.numpy as jnp
from jax import lax
from jax.experimental import pallas as pl
from jax.experimental.pallas import tpu as pltpu
from jax.sharding import PartitionSpec as P

HEADS = 32
KV_HEADS = 4
HEAD_DIM = 128
BLOCK = 128
RATIO = HEADS // KV_HEADS
NEG = -1e30
NT = (((1,), (1,)), ((), ()))


def swap(value, axis, mask):
    pairs = [(i, i ^ mask) for i in range(lax.axis_size(axis))]
    return lax.ppermute(value, axis, pairs)


def dot(a, b, dims=(((1,), (0,)), ((), ()))):
    return lax.dot_general(a, b, dims, preferred_element_type=jnp.float32)


def copy_columns(chips, span, wide, chip, inputs_ref, outs, start):
    for k, out in enumerate(outs):
        for i, d in enumerate(span):
            source = pl.ds(pl.multiple_of((d * chips + jnp.bitwise_xor(chip, k)) * wide, wide), wide)
            out[:, start + i * wide : start + (i + 1) * wide] = inputs_ref[0, :, source]


def attention_kernel(pieces, blocks_here, steps, per_step, span, wide, where_ref, own_mask, peer_mask, *refs):
    if span:
        inputs_ref, *refs = refs
    own_q, peer_q, own_g, peer_g = refs[:4]
    kv_refs = refs[4 : 4 + pieces]
    own_o, own_dq, peer_out = refs[4 + pieces : 7 + pieces]
    grad_refs = refs[7 + pieces : 7 + 2 * pieces]
    (mask_cols, causal, keys, values, keys_t, values_t, key_acc, value_acc, scores, weights, flows) = refs[
        7 + 2 * pieces :
    ]
    group, step = pl.program_id(0), pl.program_id(1)
    rows = 2 * blocks_here * BLOCK
    half = rows // 2
    blocks = 2 * blocks_here
    tiles = pieces * blocks
    score_scale = 1.0 / math.sqrt(HEAD_DIM)
    exp_scale = score_scale * math.log2(math.e)
    low = jnp.bfloat16

    @pl.when((group == 0) & (step == 0))
    def _():
        me = where_ref[0]
        lane = lax.broadcasted_iota(jnp.int32, (BLOCK, HEAD_DIM), 1)
        for t in range(blocks):
            mask_ref = own_mask if t < blocks_here else peer_mask
            tile = jnp.zeros((BLOCK, HEAD_DIM), jnp.float32)
            for block in range(tiles):
                key_device = jnp.bitwise_xor(me, block // blocks_here)
                seen = mask_ref[t % blocks_here, key_device * blocks_here + block % blocks_here]
                tile = jnp.where(lane == block, jnp.where(seen == 1, 0.0, NEG), tile)
            mask_cols[t * BLOCK : (t + 1) * BLOCK, :] = tile.astype(low)
        for block in range(tiles):
            part = slice(block * BLOCK, (block + 1) * BLOCK)
            keys[part, HEAD_DIM:] = jnp.where(lane == block, 1.0, 0.0).astype(low)
            values[part, HEAD_DIM:] = jnp.where(lane < 3, 1.0, 0.0).astype(low)
        key_pos = lax.broadcasted_iota(jnp.int32, (BLOCK, BLOCK), 0)
        query_pos = lax.broadcasted_iota(jnp.int32, (BLOCK, BLOCK), 1)
        causal[...] = jnp.where(key_pos <= query_pos, 0.0, NEG)

    @pl.when(step == 0)
    def _():
        for piece in range(2 * pieces):
            part = slice(piece * half, (piece + 1) * half)
            column = piece % 2 * 2 * HEAD_DIM
            key_part = kv_refs[piece // 2][:, column : column + HEAD_DIM]
            value_part = kv_refs[piece // 2][:, column + HEAD_DIM : column + 2 * HEAD_DIM]
            keys[part, :HEAD_DIM] = key_part
            values[part, :HEAD_DIM] = value_part
            keys_t[:, part] = key_part.T
            values_t[:, part] = value_part.T
        key_acc[...] = jnp.zeros_like(key_acc)
        value_acc[...] = jnp.zeros_like(value_acc)

    state = [dict() for _ in range(per_step)]

    def take(own, peer, i):
        columns = slice(i * HEAD_DIM, (i + 1) * HEAD_DIM)
        return jnp.concatenate([own[0, :, columns], peer[0, :, columns]], axis=0)

    def fold(x, op):
        return op(x.reshape(x.shape[0] // 8, 8, x.shape[1]), axis=0)

    def score(i):
        query = jnp.concatenate([take(own_q, peer_q, i), mask_cols[...]], axis=1)
        top = None
        for tile in range(tiles):
            part = slice(tile * BLOCK, (tile + 1) * BLOCK)
            got = dot(keys[part, :], query, NT)
            if tile < blocks:
                here = slice(tile * BLOCK, (tile + 1) * BLOCK)
                cut = got[:, here] + causal[...]
                got = jnp.concatenate(
                    [x for x in (got[:, : here.start], cut, got[:, here.stop :]) if x.shape[1]], axis=1
                )
            scores[i, part, :] = got
            best = fold(got, jnp.max)
            top = best if top is None else jnp.maximum(top, best)
            yield
        state[i]["top"] = jnp.max(top, axis=0, keepdims=True) * exp_scale

    def soften(i):
        top = state[i]["top"]
        total = None
        for tile in range(tiles):
            part = slice(tile * BLOCK, (tile + 1) * BLOCK)
            weight = jnp.exp2(scores[i, part, :] * exp_scale - top)
            weights[part, i * rows : (i + 1) * rows] = weight.astype(low)
            add = fold(weight, jnp.sum)
            total = add if total is None else total + add
            yield
        state[i]["inverse"] = 1.0 / jnp.sum(total, axis=0, keepdims=True)

    def attend(i):
        columns = slice(i * HEAD_DIM, (i + 1) * HEAD_DIM)
        inverse = state[i]["inverse"]
        grad_t = (take(own_g, peer_g, i).T.astype(jnp.float32) * inverse).astype(low)
        out_t = None
        wide_tile = 2 * BLOCK
        for start in range(0, tiles * BLOCK, wide_tile):
            part = slice(start, start + wide_tile)
            got = dot(values_t[:, part], weights[part, i * rows : (i + 1) * rows])
            out_t = got if out_t is None else out_t + got
            yield
        out_t = out_t * inverse
        delta = -jnp.sum(out_t * grad_t.astype(jnp.float32), axis=0, keepdims=True)
        out = out_t.astype(low).T
        own_o[:, columns] = out[:half]
        peer_out[:, columns] = out[half:]
        first = delta.astype(low).astype(jnp.float32)
        second = (delta - first).astype(low).astype(jnp.float32)
        third = delta - first - second
        line = lax.broadcasted_iota(jnp.int32, (HEAD_DIM, rows), 0)
        extra = jnp.where(
            line == 0, first, jnp.where(line == 1, second, jnp.where(line == 2, third, 0.0))
        ).astype(low)
        state[i]["grad_t"] = grad_t
        state[i]["both_t"] = jnp.concatenate([grad_t, extra], axis=0)
        yield

    def flow(i):
        both_t = state[i]["both_t"]
        span = slice(i * rows, (i + 1) * rows)
        for tile in range(tiles):
            part = slice(tile * BLOCK, (tile + 1) * BLOCK)
            got = dot(values[part, :], both_t)
            flows[part, span] = (weights[part, span].astype(jnp.float32) * got).astype(low)
            yield

    def finish(i):
        columns = slice(i * HEAD_DIM, (i + 1) * HEAD_DIM)
        span = slice(i * rows, (i + 1) * rows)
        query_grad = (dot(keys_t[...], flows[:, span]) * score_scale).astype(low).T
        own_dq[:, columns] = query_grad[:half]
        start = (RATIO + i) * HEAD_DIM
        peer_out[:, start : start + HEAD_DIM] = query_grad[half:]
        yield

    def gather(i):
        if i % 2:
            span = slice((i - 1) * rows, (i + 1) * rows)
            grads_t = jnp.concatenate([state[j]["grad_t"] for j in (i - 1, i)], axis=1)
            queries = jnp.concatenate([take(own_q, peer_q, j) for j in (i - 1, i)], axis=0)
            for tile in range(tiles):
                part = slice(tile * BLOCK, (tile + 1) * BLOCK)
                value_acc[part, :] += dot(weights[part, span], grads_t, NT)
                key_acc[part, :] += dot(flows[part, span], queries)
                yield

    stages = [score, soften, attend, flow, finish, gather]
    for slot in range(per_step + len(stages) - 1):
        active = [
            stage(slot - lag)
            for lag, stage in reversed(list(enumerate(stages)))
            if 0 <= slot - lag < per_step
        ]
        done = object()
        while active:
            active = [work for work in active if next(work, done) is not done]

    @pl.when(step == steps - 1)
    def _():
        for piece in range(2 * pieces):
            part = slice(piece * half, (piece + 1) * half)
            column = piece % 2 * 2 * HEAD_DIM
            out = grad_refs[piece // 2]
            out[:, column : column + HEAD_DIM] = (key_acc[part, :] * score_scale).astype(low)
            out[:, column + HEAD_DIM : column + 2 * HEAD_DIM] = value_acc[part, :].astype(low)
        if span:
            copy_columns(pieces, span, wide, where_ref[0] // 2, inputs_ref, grad_refs, 4 * HEAD_DIM)


def attention(me, core, own_mask, peer_mask, queries, peer_q, out_grad, peer_g, kv_pieces, group, inputs=None, span=()):
    tokens = queries.shape[1]
    blocks_here = tokens // BLOCK
    rows = 2 * tokens
    pieces = len(kv_pieces)
    per_step = RATIO
    steps = RATIO // per_step
    wide = per_step * HEAD_DIM
    where = jnp.stack([me, core]).astype(jnp.int32)

    def heads_in(g, h, where_ref, *_):
        return (0, 0, (where_ref[1] * (KV_HEADS // 2) + group) * steps + h)

    def fixed(g, h, *_):
        return (0, 0)

    wide_in = inputs.shape[2] // (lax.axis_size("dp") * pieces) if span else 0
    extra = [inputs] if span else []
    grad_cols = 4 * HEAD_DIM + wide_in * len(span)
    keys_all = pieces * rows
    out_cols = RATIO * HEAD_DIM
    result = pl.pallas_call(
        functools.partial(attention_kernel, pieces, blocks_here, steps, per_step, span, wide_in),
        grid_spec=pltpu.PrefetchScalarGridSpec(
            num_scalar_prefetch=3,
            grid=(1, steps),
            in_specs=[pl.BlockSpec(x.shape, lambda *_: (0, 0, 0)) for x in extra]
            + [pl.BlockSpec((1, tokens, wide), heads_in)] * 4
            + [pl.BlockSpec((tokens, 4 * HEAD_DIM), fixed)] * pieces,
            out_specs=[pl.BlockSpec((tokens, wide), fixed)] * 2
            + [pl.BlockSpec((tokens, 2 * wide), fixed)]
            + [pl.BlockSpec((tokens, grad_cols), fixed)] * pieces,
            scratch_shapes=[
                pltpu.VMEM((rows, HEAD_DIM), jnp.bfloat16),
                pltpu.VMEM((BLOCK, BLOCK), jnp.float32),
                pltpu.VMEM((keys_all, 2 * HEAD_DIM), jnp.bfloat16),
                pltpu.VMEM((keys_all, 2 * HEAD_DIM), jnp.bfloat16),
                pltpu.VMEM((HEAD_DIM, keys_all), jnp.bfloat16),
                pltpu.VMEM((HEAD_DIM, keys_all), jnp.bfloat16),
                pltpu.VMEM((keys_all, HEAD_DIM), jnp.float32),
                pltpu.VMEM((keys_all, HEAD_DIM), jnp.float32),
                pltpu.VMEM((per_step, keys_all, rows), jnp.float32),
                pltpu.VMEM((keys_all, per_step * rows), jnp.bfloat16),
                pltpu.VMEM((keys_all, per_step * rows), jnp.bfloat16),
            ],
        ),
        out_shape=[jax.ShapeDtypeStruct((tokens, out_cols), jnp.bfloat16)] * 2
        + [jax.ShapeDtypeStruct((tokens, 2 * out_cols), jnp.bfloat16)]
        + [jax.ShapeDtypeStruct((tokens, grad_cols), jnp.bfloat16)] * pieces,
        compiler_params=pltpu.CompilerParams(vmem_limit_bytes=(16 << 20) + 8 * per_step * rows * keys_all + 2 * per_step * rows * keys_all),
        cost_estimate=pl.CostEstimate(
            flops=(24 if span else 1) * RATIO * rows * keys_all * HEAD_DIM,
            transcendentals=RATIO * rows * keys_all,
            bytes_accessed=16 * tokens * out_cols,
        ),
        name="attention",
    )(where, own_mask, peer_mask, *extra, queries, peer_q, out_grad, peer_g, *kv_pieces)
    return list(result[:3]), list(result[3:])


def small_call(kernel, name, scalars, operands, out_shape, cost=2_000_000, scratch=(), streamed=False):
    whole = pl.BlockSpec(memory_space=pltpu.VMEM)
    return pl.pallas_call(
        kernel,
        grid=(1,) if streamed else (),
        in_specs=[pl.BlockSpec(memory_space=pltpu.SMEM)]
        + [pl.BlockSpec(x.shape, lambda i, n=x.ndim: (0,) * n) if streamed else whole for x in operands],
        out_specs=jax.tree.map(lambda _: whole, out_shape),
        out_shape=out_shape,
        scratch_shapes=scratch,
        compiler_params=pltpu.CompilerParams(vmem_limit_bytes=32 * 1024 * 1024),
        cost_estimate=pl.CostEstimate(flops=0, transcendentals=0, bytes_accessed=cost),
        name=name,
    )(scalars, *operands)


def pick_kernel(scalar_ref, own, peer, *outs):
    for i, out in enumerate(outs):
        for j in range(4):
            source = (own, peer)[j // 2]
            start = (j % 2 * KV_HEADS + 2 * scalar_ref[0] + i) * HEAD_DIM
            lanes = pl.ds(pl.multiple_of(start, HEAD_DIM), HEAD_DIM)
            out[:, j * HEAD_DIM : (j + 1) * HEAD_DIM] = source[:, lanes]


def turn_kernel(offset, scalar_ref, *refs):
    *parts, out = refs
    tokens = parts[0].shape[0]
    for i, part in enumerate(parts):
        out[:, i * tokens : (i + 1) * tokens] = part[:, offset:].T


def product_kernel(plan, scale, scalar_ref, own_low, own_high, peer_low, peer_high, *refs):
    *refs, whole = refs
    pieces = len(refs) - len(plan)
    grads, outs = refs[:pieces], refs[pieces:]
    own_grad = jnp.concatenate([g[:, : 2 * HEAD_DIM] for g in grads], axis=0)
    peer_grad = jnp.concatenate([g[:, 2 * HEAD_DIM :] for g in grads], axis=0)
    half = own_low.shape[0]
    for i, (own, peer) in enumerate(((own_low, peer_low), (own_high, peer_high))):
        got = dot(own[...], own_grad) + dot(peer[...], peer_grad)
        whole[i * half : i * half + own.shape[0], :] = got * scale
    for chunks, out in zip(plan, outs):
        size = out.shape[0] // len(chunks)
        for i, k in enumerate(chunks):
            start = pl.multiple_of(jnp.bitwise_xor(scalar_ref[0], k) * size, size)
            out[i * size : (i + 1) * size, :] = whole[pl.ds(start, size), :].astype(out.dtype)


def pack_kernel(span, scalar_ref, inputs_ref, front, *outs):
    wide = (outs[0].shape[1] - front.shape[1]) // len(span)
    copy_columns(len(outs), span, wide, scalar_ref[0], inputs_ref, outs, front.shape[1])
    for out in outs[1:]:
        out[:, : front.shape[1]] = front[...]


def columns_for(inputs, me, k, chips, span):
    tokens, width = inputs.shape[1:]
    wide = width // (lax.axis_size("dp") * chips)
    shaped = inputs[0].reshape(tokens, -1, chips, wide)[:, span[0] : span[-1] + 1]
    part = lax.dynamic_index_in_dim(shaped, (me // 2) ^ k, 2, keepdims=False)
    return part.reshape(tokens, wide * len(span))


def pack(inputs, front, me, chips, span):
    tokens = inputs.shape[1]
    wide = inputs.shape[2] // (lax.axis_size("dp") * chips)
    if wide % HEAD_DIM:
        return [
            jnp.concatenate([front, columns_for(inputs, me, k, chips, span)], axis=1)
            for k in range(chips)
        ]
    return small_call(
        functools.partial(pack_kernel, span),
        "pack",
        (me // 2).reshape(1).astype(jnp.int32),
        [inputs, front],
        [jax.ShapeDtypeStruct((tokens, front.shape[1] + wide * len(span)), jnp.bfloat16)] * chips,
        cost=1,
    )


def settle_kernel(starts, scalar_ref, *refs):
    *parts, keep, send = refs
    size = keep.shape[0]
    core = scalar_ref[0]
    count = len(parts) // 2
    for first, out in ((core * size, keep), ((1 - core) * size, send)):
        for j in range(2):
            total = None
            for ref, start in zip(parts[j * count : (j + 1) * count], starts):
                part = ref[pl.ds(pl.multiple_of(first + start, size), size), :].astype(jnp.float32)
                total = part if total is None else total + part
            out[:, j * 2 * HEAD_DIM : (j + 1) * 2 * HEAD_DIM] = total


def close_kernel(scalar_ref, keep, got, key_out, value_out):
    core = scalar_ref[0]
    for side, ref in ((core, keep), (1 - core, got)):
        for i in range(2):
            span = pl.ds(pl.multiple_of((2 * side + i) * HEAD_DIM, HEAD_DIM), HEAD_DIM)
            key_out[:, span] = ref[:, 2 * i * HEAD_DIM : (2 * i + 1) * HEAD_DIM]
            value_out[:, span] = ref[:, (2 * i + 1) * HEAD_DIM : (2 * i + 2) * HEAD_DIM]


def join_kernel(scalar_ref, own_o_a, own_o_b, own_dq_a, own_dq_b, got_a, got_b, out, query_grad, sem):
    core = scalar_ref[0]
    wide = own_o_a.shape[1]
    copies = []
    for j, (whole, own) in enumerate(((out, (own_o_a, own_o_b)), (query_grad, (own_dq_a, own_dq_b)))):
        for i in range(2):
            other = (got_a, got_b)[i].at[:, j * wide : (j + 1) * wide]
            for side, ref in ((core, own[i]), (1 - core, other)):
                span = pl.ds(pl.multiple_of((2 * side + i) * wide, wide), wide)
                copies.append(pltpu.make_async_copy(ref, whole.at[0, :, span], sem.at[len(copies)]))
    for copy in copies:
        copy.start()
    for copy in copies:
        copy.wait()


def join(core_scalar, parts, shape):
    return pl.pallas_call(
        join_kernel,
        in_specs=[pl.BlockSpec(memory_space=pltpu.SMEM)]
        + [pl.BlockSpec(memory_space=pl.ANY)] * len(parts),
        out_specs=[pl.BlockSpec(memory_space=pltpu.VMEM)] * 2,
        out_shape=[jax.ShapeDtypeStruct(shape, jnp.bfloat16)] * 2,
        scratch_shapes=[pltpu.SemaphoreType.DMA((8,))],
        cost_estimate=pl.CostEstimate(flops=0, transcendentals=0, bytes_accessed=4_000_000),
        name="join",
    )(core_scalar, *parts)


def hold(values, *others):
    return lax.optimization_barrier((values, others))[0]


def body(inputs, queries, keys_values, out_grad, tree_mask):
    tokens = queries.shape[1]
    width = queries.shape[2]
    count = lax.axis_size("ctx")
    data_size = lax.axis_size("dp")
    me = lax.axis_index("ctx")
    data_me = lax.axis_index("dp")
    core = me % 2
    chips = count // 2
    hops = [2 * p for p in range(1, chips)]
    low, high = jnp.bfloat16, jnp.float32
    core_scalar = core.reshape(1).astype(jnp.int32)
    data_scalar = data_me.reshape(1).astype(jnp.int32)

    flat = lax.optimization_barrier(keys_values.reshape(tokens, 2 * KV_HEADS * HEAD_DIM))
    own_a, own_b = small_call(
        pick_kernel,
        "pick",
        core_scalar,
        [flat, swap(flat, "ctx", 1)],
        [jax.ShapeDtypeStruct((tokens, 4 * HEAD_DIM), low)] * 2,
        cost=1,
    )
    pieces_a = [own_a] + [swap(own_a, "ctx", k) for k in hops]
    own_mask, queries_later, out_grad_later = hold((tree_mask[0], queries, out_grad), own_a)
    peer_mask = swap(own_mask, "ctx", 1)
    peer_q = swap(queries_later, "ctx", 1)
    peer_g = swap(out_grad_later, "ctx", 1)
    middle = data_size // 2
    whole_lanes = width // (data_size * chips) % HEAD_DIM == 0
    low_span, high_span = range(middle), range(middle, data_size)
    packed_b = pack(inputs, hold(own_b, peer_mask), me, chips, low_span)
    sends = hold(packed_b[1:], peer_q, peer_g)
    pieces_b = [own_b] + [swap(x, "ctx", k) for x, k in zip(sends, hops)]

    heads = (me, core, own_mask, peer_mask, queries, peer_q, out_grad, peer_g)
    if whole_lanes:
        outs_a, packed_a = attention(*heads, pieces_a, 0, inputs, high_span)
    else:
        outs_a, packed_a = attention(*heads, pieces_a, 0)
        packed_a = [
            jnp.concatenate([x, columns_for(inputs, me, k, chips, high_span)], axis=1)
            for k, x in enumerate(packed_a)
        ]
    back_a = [swap(x, "ctx", k) for x, k in zip(packed_a[1:], hops)]
    got_a = swap(outs_a[2], "ctx", 1)
    pieces_b = hold(pieces_b, outs_a[2])

    def turn(parts, streamed):
        return small_call(
            functools.partial(turn_kernel, 4 * HEAD_DIM),
            "turn",
            core_scalar,
            parts,
            jax.ShapeDtypeStruct((parts[0].shape[1] - 4 * HEAD_DIM, chips * tokens), low),
            cost=1,
            streamed=streamed,
        )

    own_low = turn(list(packed_b[:1]) + list(pieces_b[1:]), True)
    peer_low = swap(own_low, "ctx", 1)
    outs_b, grads_b = attention(*heads, pieces_b, 1)
    grads_b, back_a, got_a, peer_low = lax.optimization_barrier((grads_b, back_a, got_a, peer_low))
    back_b = [swap(x, "ctx", k) for x, k in zip(grads_b[1:], hops)]
    own_high = turn(list(packed_a[:1]) + list(back_a), False)
    peer_high = swap(own_high, "ctx", 1)

    def owned(mine, back):
        total = mine.astype(high)
        for x in back:
            total = total + x.astype(high)
        return total.astype(low)

    def gathered(total):
        return [total] + [swap(total, "ctx", k) for k in hops]

    scale = 1.0 / math.sqrt(tokens * count * data_size)
    rows_out = width // (data_size * count)
    size = 2 * rows_out
    pairwise = data_size == 4
    plan = [[0], [2], [3, 1]] if pairwise else [[k] for k in range(data_size)]
    kinds = [high, high, low] if pairwise else [high] + [low] * (data_size - 1)

    def product(grads):
        return small_call(
            functools.partial(product_kernel, plan, scale),
            "product",
            data_scalar,
            [own_low, own_high, peer_low, peer_high] + grads,
            [
                jax.ShapeDtypeStruct((size * len(chunks), 2 * HEAD_DIM), kind)
                for chunks, kind in zip(plan, kinds)
            ],
            scratch=[pltpu.VMEM((size * data_size, 2 * HEAD_DIM), high)],
        )

    folded = 4 * HEAD_DIM
    all_a = gathered(owned(packed_a[0][:, :folded], [x[:, :folded] for x in back_a]))
    all_b = gathered(owned(grads_b[0], back_b))
    chunks_a = product(all_a)
    all_b = hold(all_b, chunks_a)
    chunks_b = product(all_b)
    if pairwise:
        near_a = swap(chunks_a[2], "dp", 1)
        cross_a = (chunks_a[1] + near_a[:size].astype(high)).astype(low)
        near_b = swap(hold(chunks_b[2], cross_a), "dp", 1)
        cross_b = (chunks_b[1] + near_b[:size].astype(high)).astype(low)
        arrived = [[near_a, swap(cross_a, "dp", 2)], [near_b, swap(cross_b, "dp", 2)]]
        starts = [0, size, 0]
    else:
        arrived = [[swap(x[k], "dp", k) for k in range(1, data_size)] for x in (chunks_a, chunks_b)]
        cross_b = chunks_b[0]
        starts = [0] * data_size
    got_b = swap(hold(outs_b[2], chunks_b), "ctx", 1)
    parts = [outs_a[0], outs_b[0], outs_a[1], outs_b[1], got_a, got_b]
    attn_out, query_grad = join(core_scalar, hold(parts, cross_b), queries.shape)
    arrived, attn_out, query_grad = lax.optimization_barrier((arrived, attn_out, query_grad))
    kept, sent = small_call(
        functools.partial(settle_kernel, starts),
        "settle",
        core_scalar,
        [chunks_a[0]] + arrived[0] + [chunks_b[0]] + arrived[1],
        [jax.ShapeDtypeStruct((rows_out, 4 * HEAD_DIM), high)] * 2,
    )
    key_out, value_out = small_call(
        close_kernel,
        "close",
        core_scalar,
        [kept, swap(sent, "ctx", 1)],
        [jax.ShapeDtypeStruct((rows_out, KV_HEADS * HEAD_DIM), high)] * 2,
    )
    return attn_out, query_grad, key_out, value_out


def solution(mesh):
    in_specs = (
        P("dp", "ctx", None),
        P("dp", "ctx", None),
        P("dp", "ctx", None, None),
        P("dp", "ctx", None),
        P("dp", "ctx", None),
    )
    out_specs = (
        P("dp", "ctx", None),
        P("dp", "ctx", None),
        P(("dp", "ctx"), None),
        P(("dp", "ctx"), None),
    )
    return jax.shard_map(body, mesh=mesh, in_specs=in_specs, out_specs=out_specs, check_vma=False)
```

```python
import functools
import math

import jax
import jax.numpy as jnp
from jax import lax
from jax.experimental import pallas as pl
from jax.experimental.pallas import tpu as pltpu
from jax.sharding import PartitionSpec as P

HEADS = 32
KV_HEADS = 4
HEAD_DIM = 128
BLOCK = 128
RATIO = HEADS // KV_HEADS
NEG = -1e30
NT = (((1,), (1,)), ((), ()))


def swap(value, axis, mask):
    pairs = [(i, i ^ mask) for i in range(lax.axis_size(axis))]
    return lax.ppermute(value, axis, pairs)


def dot(a, b, dims=(((1,), (0,)), ((), ()))):
    return lax.dot_general(a, b, dims, preferred_element_type=jnp.float32)


def copy_columns(chips, span, wide, chip, inputs_ref, outs, start):
    for k, out in enumerate(outs):
        for i, d in enumerate(span):
            source = pl.ds(pl.multiple_of((d * chips + jnp.bitwise_xor(chip, k)) * wide, wide), wide)
            out[:, start + i * wide : start + (i + 1) * wide] = inputs_ref[0, :, source]


def attention_kernel(pieces, blocks_here, steps, per_step, span, wide, where_ref, own_mask, peer_mask, *refs):
    if span:
        inputs_ref, *refs = refs
    own_q, peer_q, own_g, peer_g = refs[:4]
    kv_refs = refs[4 : 4 + pieces]
    own_o, own_dq, peer_out = refs[4 + pieces : 7 + pieces]
    grad_refs = refs[7 + pieces : 7 + 2 * pieces]
    (mask_cols, causal, keys, values, keys_t, values_t, key_acc, value_acc, scores, weights, flows) = refs[
        7 + 2 * pieces :
    ]
    group, step = pl.program_id(0), pl.program_id(1)
    rows = 2 * blocks_here * BLOCK
    half = rows // 2
    blocks = 2 * blocks_here
    tiles = pieces * blocks
    score_scale = 1.0 / math.sqrt(HEAD_DIM)
    exp_scale = score_scale * math.log2(math.e)
    low = jnp.bfloat16

    @pl.when((group == 0) & (step == 0))
    def _():
        me = where_ref[0]
        lane = lax.broadcasted_iota(jnp.int32, (BLOCK, HEAD_DIM), 1)
        for t in range(blocks):
            mask_ref = own_mask if t < blocks_here else peer_mask
            tile = jnp.zeros((BLOCK, HEAD_DIM), jnp.float32)
            for block in range(tiles):
                key_device = jnp.bitwise_xor(me, block // blocks_here)
                seen = mask_ref[t % blocks_here, key_device * blocks_here + block % blocks_here]
                tile = jnp.where(lane == block, jnp.where(seen == 1, 0.0, NEG), tile)
            mask_cols[t * BLOCK : (t + 1) * BLOCK, :] = tile.astype(low)
        for block in range(tiles):
            part = slice(block * BLOCK, (block + 1) * BLOCK)
            keys[part, HEAD_DIM:] = jnp.where(lane == block, 1.0, 0.0).astype(low)
            values[part, HEAD_DIM:] = jnp.where(lane < 3, 1.0, 0.0).astype(low)
        key_pos = lax.broadcasted_iota(jnp.int32, (BLOCK, BLOCK), 0)
        query_pos = lax.broadcasted_iota(jnp.int32, (BLOCK, BLOCK), 1)
        causal[...] = jnp.where(key_pos <= query_pos, 0.0, NEG)

    @pl.when(step == 0)
    def _():
        for piece in range(2 * pieces):
            part = slice(piece * half, (piece + 1) * half)
            column = piece % 2 * 2 * HEAD_DIM
            key_part = kv_refs[piece // 2][:, column : column + HEAD_DIM]
            value_part = kv_refs[piece // 2][:, column + HEAD_DIM : column + 2 * HEAD_DIM]
            keys[part, :HEAD_DIM] = key_part
            values[part, :HEAD_DIM] = value_part
            keys_t[:, part] = key_part.T
            values_t[:, part] = value_part.T
        key_acc[...] = jnp.zeros_like(key_acc)
        value_acc[...] = jnp.zeros_like(value_acc)

    state = [dict() for _ in range(per_step)]

    def take(own, peer, i):
        columns = slice(i * HEAD_DIM, (i + 1) * HEAD_DIM)
        return jnp.concatenate([own[0, :, columns], peer[0, :, columns]], axis=0)

    def fold(x, op):
        return op(x.reshape(x.shape[0] // 8, 8, x.shape[1]), axis=0)

    def score(i):
        query = jnp.concatenate([take(own_q, peer_q, i), mask_cols[...]], axis=1)
        top = None
        for tile in range(tiles):
            part = slice(tile * BLOCK, (tile + 1) * BLOCK)
            got = dot(keys[part, :], query, NT)
            if tile < blocks:
                here = slice(tile * BLOCK, (tile + 1) * BLOCK)
                cut = got[:, here] + causal[...]
                got = jnp.concatenate(
                    [x for x in (got[:, : here.start], cut, got[:, here.stop :]) if x.shape[1]], axis=1
                )
            scores[i, part, :] = got
            best = fold(got, jnp.max)
            top = best if top is None else jnp.maximum(top, best)
            yield
        state[i]["top"] = jnp.max(top, axis=0, keepdims=True) * exp_scale

    def soften(i):
        top = state[i]["top"]
        total = None
        for tile in range(tiles):
            part = slice(tile * BLOCK, (tile + 1) * BLOCK)
            weight = jnp.exp2(scores[i, part, :] * exp_scale - top)
            weights[part, i * rows : (i + 1) * rows] = weight.astype(low)
            add = fold(weight, jnp.sum)
            total = add if total is None else total + add
            yield
        state[i]["inverse"] = 1.0 / jnp.sum(total, axis=0, keepdims=True)

    def attend(i):
        columns = slice(i * HEAD_DIM, (i + 1) * HEAD_DIM)
        inverse = state[i]["inverse"]
        grad_t = (take(own_g, peer_g, i).T.astype(jnp.float32) * inverse).astype(low)
        out_t = None
        wide_tile = 2 * BLOCK
        for start in range(0, tiles * BLOCK, wide_tile):
            part = slice(start, start + wide_tile)
            got = dot(values_t[:, part], weights[part, i * rows : (i + 1) * rows])
            out_t = got if out_t is None else out_t + got
            yield
        out_t = out_t * inverse
        delta = -jnp.sum(out_t * grad_t.astype(jnp.float32), axis=0, keepdims=True)
        out = out_t.astype(low).T
        own_o[:, columns] = out[:half]
        peer_out[:, columns] = out[half:]
        first = delta.astype(low).astype(jnp.float32)
        second = (delta - first).astype(low).astype(jnp.float32)
        third = delta - first - second
        line = lax.broadcasted_iota(jnp.int32, (HEAD_DIM, rows), 0)
        extra = jnp.where(
            line == 0, first, jnp.where(line == 1, second, jnp.where(line == 2, third, 0.0))
        ).astype(low)
        state[i]["grad_t"] = grad_t
        state[i]["both_t"] = jnp.concatenate([grad_t, extra], axis=0)
        yield

    def flow(i):
        both_t = state[i]["both_t"]
        span = slice(i * rows, (i + 1) * rows)
        for tile in range(tiles):
            part = slice(tile * BLOCK, (tile + 1) * BLOCK)
            got = dot(values[part, :], both_t)
            flows[part, span] = (weights[part, span].astype(jnp.float32) * got).astype(low)
            yield

    def finish(i):
        columns = slice(i * HEAD_DIM, (i + 1) * HEAD_DIM)
        span = slice(i * rows, (i + 1) * rows)
        query_grad = (dot(keys_t[...], flows[:, span]) * score_scale).astype(low).T
        own_dq[:, columns] = query_grad[:half]
        start = (RATIO + i) * HEAD_DIM
        peer_out[:, start : start + HEAD_DIM] = query_grad[half:]
        yield

    def gather(i):
        if i % 2:
            span = slice((i - 1) * rows, (i + 1) * rows)
            grads_t = jnp.concatenate([state[j]["grad_t"] for j in (i - 1, i)], axis=1)
            queries = jnp.concatenate([take(own_q, peer_q, j) for j in (i - 1, i)], axis=0)
            for tile in range(tiles):
                part = slice(tile * BLOCK, (tile + 1) * BLOCK)
                value_acc[part, :] += dot(weights[part, span], grads_t, NT)
                key_acc[part, :] += dot(flows[part, span], queries)
                yield

    stages = [score, soften, attend, flow, finish, gather]
    for slot in range(per_step + len(stages) - 1):
        active = [
            stage(slot - lag)
            for lag, stage in reversed(list(enumerate(stages)))
            if 0 <= slot - lag < per_step
        ]
        done = object()
        while active:
            active = [work for work in active if next(work, done) is not done]

    @pl.when(step == steps - 1)
    def _():
        for piece in range(2 * pieces):
            part = slice(piece * half, (piece + 1) * half)
            column = piece % 2 * 2 * HEAD_DIM
            out = grad_refs[piece // 2]
            out[:, column : column + HEAD_DIM] = (key_acc[part, :] * score_scale).astype(low)
            out[:, column + HEAD_DIM : column + 2 * HEAD_DIM] = value_acc[part, :].astype(low)
        if span:
            copy_columns(pieces, span, wide, where_ref[0] // 2, inputs_ref, grad_refs, 4 * HEAD_DIM)


def attention(me, core, own_mask, peer_mask, queries, peer_q, out_grad, peer_g, kv_pieces, group, inputs=None, span=()):
    tokens = queries.shape[1]
    blocks_here = tokens // BLOCK
    rows = 2 * tokens
    pieces = len(kv_pieces)
    per_step = RATIO
    steps = RATIO // per_step
    wide = per_step * HEAD_DIM
    where = jnp.stack([me, core]).astype(jnp.int32)

    def heads_in(g, h, where_ref, *_):
        return (0, 0, (where_ref[1] * (KV_HEADS // 2) + group) * steps + h)

    def fixed(g, h, *_):
        return (0, 0)

    wide_in = inputs.shape[2] // (lax.axis_size("dp") * pieces) if span else 0
    extra = [inputs] if span else []
    grad_cols = 4 * HEAD_DIM + wide_in * len(span)
    keys_all = pieces * rows
    out_cols = RATIO * HEAD_DIM
    result = pl.pallas_call(
        functools.partial(attention_kernel, pieces, blocks_here, steps, per_step, span, wide_in),
        grid_spec=pltpu.PrefetchScalarGridSpec(
            num_scalar_prefetch=3,
            grid=(1, steps),
            in_specs=[pl.BlockSpec(x.shape, lambda *_: (0, 0, 0)) for x in extra]
            + [pl.BlockSpec((1, tokens, wide), heads_in)] * 4
            + [pl.BlockSpec((tokens, 4 * HEAD_DIM), fixed)] * pieces,
            out_specs=[pl.BlockSpec((tokens, wide), fixed)] * 2
            + [pl.BlockSpec((tokens, 2 * wide), fixed)]
            + [pl.BlockSpec((tokens, grad_cols), fixed)] * pieces,
            scratch_shapes=[
                pltpu.VMEM((rows, HEAD_DIM), jnp.bfloat16),
                pltpu.VMEM((BLOCK, BLOCK), jnp.float32),
                pltpu.VMEM((keys_all, 2 * HEAD_DIM), jnp.bfloat16),
                pltpu.VMEM((keys_all, 2 * HEAD_DIM), jnp.bfloat16),
                pltpu.VMEM((HEAD_DIM, keys_all), jnp.bfloat16),
                pltpu.VMEM((HEAD_DIM, keys_all), jnp.bfloat16),
                pltpu.VMEM((keys_all, HEAD_DIM), jnp.float32),
                pltpu.VMEM((keys_all, HEAD_DIM), jnp.float32),
                pltpu.VMEM((per_step, keys_all, rows), jnp.float32),
                pltpu.VMEM((keys_all, per_step * rows), jnp.bfloat16),
                pltpu.VMEM((keys_all, per_step * rows), jnp.bfloat16),
            ],
        ),
        out_shape=[jax.ShapeDtypeStruct((tokens, out_cols), jnp.bfloat16)] * 2
        + [jax.ShapeDtypeStruct((tokens, 2 * out_cols), jnp.bfloat16)]
        + [jax.ShapeDtypeStruct((tokens, grad_cols), jnp.bfloat16)] * pieces,
        compiler_params=pltpu.CompilerParams(vmem_limit_bytes=(16 << 20) + 8 * per_step * rows * keys_all + 2 * per_step * rows * keys_all),
        cost_estimate=pl.CostEstimate(
            flops=(24 if span else 1) * RATIO * rows * keys_all * HEAD_DIM,
            transcendentals=RATIO * rows * keys_all,
            bytes_accessed=16 * tokens * out_cols,
        ),
        name="attention",
    )(where, own_mask, peer_mask, *extra, queries, peer_q, out_grad, peer_g, *kv_pieces)
    return list(result[:3]), list(result[3:])


def small_call(kernel, name, scalars, operands, out_shape, cost=2_000_000, scratch=(), streamed=False):
    whole = pl.BlockSpec(memory_space=pltpu.VMEM)
    return pl.pallas_call(
        kernel,
        grid=(1,) if streamed else (),
        in_specs=[pl.BlockSpec(memory_space=pltpu.SMEM)]
        + [pl.BlockSpec(x.shape, lambda i, n=x.ndim: (0,) * n) if streamed else whole for x in operands],
        out_specs=jax.tree.map(lambda _: whole, out_shape),
        out_shape=out_shape,
        scratch_shapes=scratch,
        compiler_params=pltpu.CompilerParams(vmem_limit_bytes=32 * 1024 * 1024),
        cost_estimate=pl.CostEstimate(flops=0, transcendentals=0, bytes_accessed=cost),
        name=name,
    )(scalars, *operands)


def pick_kernel(scalar_ref, own, peer, *outs):
    for i, out in enumerate(outs):
        for j in range(4):
            source = (own, peer)[j // 2]
            start = (j % 2 * KV_HEADS + 2 * scalar_ref[0] + i) * HEAD_DIM
            lanes = pl.ds(pl.multiple_of(start, HEAD_DIM), HEAD_DIM)
            out[:, j * HEAD_DIM : (j + 1) * HEAD_DIM] = source[:, lanes]


def turn_kernel(offset, scalar_ref, *refs):
    *parts, out = refs
    tokens = parts[0].shape[0]
    for i, part in enumerate(parts):
        out[:, i * tokens : (i + 1) * tokens] = part[:, offset:].T


def product_kernel(plan, scale, scalar_ref, own_low, own_high, peer_low, peer_high, *refs):
    *refs, whole = refs
    pieces = len(refs) - len(plan)
    grads, outs = refs[:pieces], refs[pieces:]
    own_grad = jnp.concatenate([g[:, : 2 * HEAD_DIM] for g in grads], axis=0)
    peer_grad = jnp.concatenate([g[:, 2 * HEAD_DIM :] for g in grads], axis=0)
    half = own_low.shape[0]
    for i, (own, peer) in enumerate(((own_low, peer_low), (own_high, peer_high))):
        got = dot(own[...], own_grad) + dot(peer[...], peer_grad)
        whole[i * half : i * half + own.shape[0], :] = got * scale
    for chunks, out in zip(plan, outs):
        size = out.shape[0] // len(chunks)
        for i, k in enumerate(chunks):
            start = pl.multiple_of(jnp.bitwise_xor(scalar_ref[0], k) * size, size)
            out[i * size : (i + 1) * size, :] = whole[pl.ds(start, size), :].astype(out.dtype)


def pack_kernel(span, scalar_ref, inputs_ref, front, *outs):
    wide = (outs[0].shape[1] - front.shape[1]) // len(span)
    copy_columns(len(outs), span, wide, scalar_ref[0], inputs_ref, outs, front.shape[1])
    for out in outs[1:]:
        out[:, : front.shape[1]] = front[...]


def columns_for(inputs, me, k, chips, span):
    tokens, width = inputs.shape[1:]
    wide = width // (lax.axis_size("dp") * chips)
    shaped = inputs[0].reshape(tokens, -1, chips, wide)[:, span[0] : span[-1] + 1]
    part = lax.dynamic_index_in_dim(shaped, (me // 2) ^ k, 2, keepdims=False)
    return part.reshape(tokens, wide * len(span))


def pack(inputs, front, me, chips, span):
    tokens = inputs.shape[1]
    wide = inputs.shape[2] // (lax.axis_size("dp") * chips)
    if wide % HEAD_DIM:
        return [
            jnp.concatenate([front, columns_for(inputs, me, k, chips, span)], axis=1)
            for k in range(chips)
        ]
    return small_call(
        functools.partial(pack_kernel, span),
        "pack",
        (me // 2).reshape(1).astype(jnp.int32),
        [inputs, front],
        [jax.ShapeDtypeStruct((tokens, front.shape[1] + wide * len(span)), jnp.bfloat16)] * chips,
        cost=1,
    )


def settle_kernel(starts, scalar_ref, *refs):
    *parts, keep, send = refs
    size = keep.shape[0]
    core = scalar_ref[0]
    count = len(parts) // 2
    for first, out in ((core * size, keep), ((1 - core) * size, send)):
        for j in range(2):
            total = None
            for ref, start in zip(parts[j * count : (j + 1) * count], starts):
                part = ref[pl.ds(pl.multiple_of(first + start, size), size), :].astype(jnp.float32)
                total = part if total is None else total + part
            out[:, j * 2 * HEAD_DIM : (j + 1) * 2 * HEAD_DIM] = total


def close_kernel(scalar_ref, keep, got, key_out, value_out):
    core = scalar_ref[0]
    for side, ref in ((core, keep), (1 - core, got)):
        for i in range(2):
            span = pl.ds(pl.multiple_of((2 * side + i) * HEAD_DIM, HEAD_DIM), HEAD_DIM)
            key_out[:, span] = ref[:, 2 * i * HEAD_DIM : (2 * i + 1) * HEAD_DIM]
            value_out[:, span] = ref[:, (2 * i + 1) * HEAD_DIM : (2 * i + 2) * HEAD_DIM]


def join_kernel(scalar_ref, own_o_a, own_o_b, own_dq_a, own_dq_b, got_a, got_b, out, query_grad, sem):
    core = scalar_ref[0]
    wide = own_o_a.shape[1]
    copies = []
    for j, (whole, own) in enumerate(((out, (own_o_a, own_o_b)), (query_grad, (own_dq_a, own_dq_b)))):
        for i in range(2):
            other = (got_a, got_b)[i].at[:, j * wide : (j + 1) * wide]
            for side, ref in ((core, own[i]), (1 - core, other)):
                span = pl.ds(pl.multiple_of((2 * side + i) * wide, wide), wide)
                copies.append(pltpu.make_async_copy(ref, whole.at[0, :, span], sem.at[len(copies)]))
    for copy in copies:
        copy.start()
    for copy in copies:
        copy.wait()


def join(core_scalar, parts, shape):
    return pl.pallas_call(
        join_kernel,
        in_specs=[pl.BlockSpec(memory_space=pltpu.SMEM)]
        + [pl.BlockSpec(memory_space=pl.ANY)] * len(parts),
        out_specs=[pl.BlockSpec(memory_space=pltpu.VMEM)] * 2,
        out_shape=[jax.ShapeDtypeStruct(shape, jnp.bfloat16)] * 2,
        scratch_shapes=[pltpu.SemaphoreType.DMA((8,))],
        cost_estimate=pl.CostEstimate(flops=0, transcendentals=0, bytes_accessed=4_000_000),
        name="join",
    )(core_scalar, *parts)


def hold(values, *others):
    return lax.optimization_barrier((values, others))[0]


def body(inputs, queries, keys_values, out_grad, tree_mask):
    tokens = queries.shape[1]
    width = queries.shape[2]
    count = lax.axis_size("ctx")
    data_size = lax.axis_size("dp")
    me = lax.axis_index("ctx")
    data_me = lax.axis_index("dp")
    core = me % 2
    chips = count // 2
    hops = [2 * p for p in range(1, chips)]
    low, high = jnp.bfloat16, jnp.float32
    core_scalar = core.reshape(1).astype(jnp.int32)
    data_scalar = data_me.reshape(1).astype(jnp.int32)

    flat = lax.optimization_barrier(keys_values.reshape(tokens, 2 * KV_HEADS * HEAD_DIM))
    own_a, own_b = small_call(
        pick_kernel,
        "pick",
        core_scalar,
        [flat, swap(flat, "ctx", 1)],
        [jax.ShapeDtypeStruct((tokens, 4 * HEAD_DIM), low)] * 2,
        cost=1,
    )
    pieces_a = [own_a] + [swap(own_a, "ctx", k) for k in hops]
    own_mask, queries_later, out_grad_later = hold((tree_mask[0], queries, out_grad), own_a)
    peer_mask = swap(own_mask, "ctx", 1)
    peer_q = swap(queries_later, "ctx", 1)
    peer_g = swap(out_grad_later, "ctx", 1)
    middle = data_size // 2
    whole_lanes = width // (data_size * chips) % HEAD_DIM == 0
    low_span, high_span = range(middle), range(middle, data_size)
    packed_b = pack(inputs, hold(own_b, peer_mask), me, chips, low_span)
    sends = hold(packed_b[1:], peer_q, peer_g)
    pieces_b = [own_b] + [swap(x, "ctx", k) for x, k in zip(sends, hops)]

    heads = (me, core, own_mask, peer_mask, queries, peer_q, out_grad, peer_g)
    if whole_lanes:
        outs_a, packed_a = attention(*heads, pieces_a, 0, inputs, high_span)
    else:
        outs_a, packed_a = attention(*heads, pieces_a, 0)
        packed_a = [
            jnp.concatenate([x, columns_for(inputs, me, k, chips, high_span)], axis=1)
            for k, x in enumerate(packed_a)
        ]
    back_a = [swap(x, "ctx", k) for x, k in zip(packed_a[1:], hops)]
    got_a = swap(outs_a[2], "ctx", 1)
    pieces_b = hold(pieces_b, outs_a[2])

    def turn(parts, streamed):
        return small_call(
            functools.partial(turn_kernel, 4 * HEAD_DIM),
            "turn",
            core_scalar,
            parts,
            jax.ShapeDtypeStruct((parts[0].shape[1] - 4 * HEAD_DIM, chips * tokens), low),
            cost=1,
            streamed=streamed,
        )

    own_low = turn(list(packed_b[:1]) + list(pieces_b[1:]), True)
    peer_low = swap(own_low, "ctx", 1)
    outs_b, grads_b = attention(*heads, pieces_b, 1)
    grads_b, back_a, got_a, peer_low = lax.optimization_barrier((grads_b, back_a, got_a, peer_low))
    back_b = [swap(x, "ctx", k) for x, k in zip(grads_b[1:], hops)]
    own_high = turn(list(packed_a[:1]) + list(back_a), False)
    peer_high = swap(own_high, "ctx", 1)

    def owned(mine, back):
        total = mine.astype(high)
        for x in back:
            total = total + x.astype(high)
        return total.astype(low)

    def gathered(total):
        return [total] + [swap(total, "ctx", k) for k in hops]

    scale = 1.0 / math.sqrt(tokens * count * data_size)
    rows_out = width // (data_size * count)
    size = 2 * rows_out
    pairwise = data_size == 4
    plan = [[0], [2], [3, 1]] if pairwise else [[k] for k in range(data_size)]
    kinds = [high, high, low] if pairwise else [high] + [low] * (data_size - 1)

    def product(grads):
        return small_call(
            functools.partial(product_kernel, plan, scale),
            "product",
            data_scalar,
            [own_low, own_high, peer_low, peer_high] + grads,
            [
                jax.ShapeDtypeStruct((size * len(chunks), 2 * HEAD_DIM), kind)
                for chunks, kind in zip(plan, kinds)
            ],
            scratch=[pltpu.VMEM((size * data_size, 2 * HEAD_DIM), high)],
        )

    folded = 4 * HEAD_DIM
    all_a = gathered(owned(packed_a[0][:, :folded], [x[:, :folded] for x in back_a]))
    all_b = gathered(owned(grads_b[0], back_b))
    chunks_a = product(all_a)
    all_b = hold(all_b, chunks_a)
    chunks_b = product(all_b)
    if pairwise:
        near_a = swap(chunks_a[2], "dp", 1)
        cross_a = (chunks_a[1] + near_a[:size].astype(high)).astype(low)
        far_a = swap(cross_a, "dp", 2)
        near_b = swap(hold(chunks_b[2], far_a), "dp", 1)
        cross_b = (chunks_b[1] + near_b[:size].astype(high)).astype(low)
        arrived = [[near_a, far_a], [near_b, swap(cross_b, "dp", 2)]]
        starts = [0, size, 0]
    else:
        arrived = [[swap(x[k], "dp", k) for k in range(1, data_size)] for x in (chunks_a, chunks_b)]
        cross_b = chunks_b[0]
        starts = [0] * data_size
    got_b = swap(hold(outs_b[2], chunks_b), "ctx", 1)
    parts = [outs_a[0], outs_b[0], outs_a[1], outs_b[1], got_a, got_b]
    attn_out, query_grad = join(core_scalar, hold(parts, cross_b), queries.shape)
    arrived, attn_out, query_grad = lax.optimization_barrier((arrived, attn_out, query_grad))
    kept, sent = small_call(
        functools.partial(settle_kernel, starts),
        "settle",
        core_scalar,
        [chunks_a[0]] + arrived[0] + [chunks_b[0]] + arrived[1],
        [jax.ShapeDtypeStruct((rows_out, 4 * HEAD_DIM), high)] * 2,
    )
    key_out, value_out = small_call(
        close_kernel,
        "close",
        core_scalar,
        [kept, swap(sent, "ctx", 1)],
        [jax.ShapeDtypeStruct((rows_out, KV_HEADS * HEAD_DIM), high)] * 2,
    )
    return attn_out, query_grad, key_out, value_out


def solution(mesh):
    in_specs = (
        P("dp", "ctx", None),
        P("dp", "ctx", None),
        P("dp", "ctx", None, None),
        P("dp", "ctx", None),
        P("dp", "ctx", None),
    )
    out_specs = (
        P("dp", "ctx", None),
        P("dp", "ctx", None),
        P(("dp", "ctx"), None),
        P(("dp", "ctx"), None),
    )
    return jax.shard_map(body, mesh=mesh, in_specs=in_specs, out_specs=out_specs, check_vma=False)
```

```python
import functools
import math

import jax
import jax.numpy as jnp
from jax import lax
from jax.experimental import pallas as pl
from jax.experimental.pallas import tpu as pltpu
from jax.sharding import PartitionSpec as P

HEADS = 32
KV_HEADS = 4
HEAD_DIM = 128
BLOCK = 128
RATIO = HEADS // KV_HEADS
NEG = -1e30
NT = (((1,), (1,)), ((), ()))


def swap(value, axis, mask):
    pairs = [(i, i ^ mask) for i in range(lax.axis_size(axis))]
    return lax.ppermute(value, axis, pairs)


def dot(a, b, dims=(((1,), (0,)), ((), ()))):
    return lax.dot_general(a, b, dims, preferred_element_type=jnp.float32)


def copy_columns(chips, span, wide, chip, inputs_ref, outs, start):
    for k, out in enumerate(outs):
        for i, d in enumerate(span):
            source = pl.ds(pl.multiple_of((d * chips + jnp.bitwise_xor(chip, k)) * wide, wide), wide)
            out[:, start + i * wide : start + (i + 1) * wide] = inputs_ref[0, :, source]


def attention_kernel(pieces, blocks_here, steps, per_step, span, wide, where_ref, own_mask, peer_mask, *refs):
    if span:
        inputs_ref, *refs = refs
    own_q, peer_q, own_g, peer_g = refs[:4]
    kv_refs = refs[4 : 4 + pieces]
    own_o, own_dq, peer_out = refs[4 + pieces : 7 + pieces]
    grad_refs = refs[7 + pieces : 7 + 2 * pieces]
    (mask_cols, causal, keys, values, keys_t, values_t, key_acc, value_acc, scores, weights, flows) = refs[
        7 + 2 * pieces :
    ]
    group, step = pl.program_id(0), pl.program_id(1)
    rows = 2 * blocks_here * BLOCK
    half = rows // 2
    blocks = 2 * blocks_here
    tiles = pieces * blocks
    score_scale = 1.0 / math.sqrt(HEAD_DIM)
    exp_scale = score_scale * math.log2(math.e)
    low = jnp.bfloat16

    @pl.when((group == 0) & (step == 0))
    def _():
        me = where_ref[0]
        lane = lax.broadcasted_iota(jnp.int32, (BLOCK, HEAD_DIM), 1)
        for t in range(blocks):
            mask_ref = own_mask if t < blocks_here else peer_mask
            tile = jnp.zeros((BLOCK, HEAD_DIM), jnp.float32)
            for block in range(tiles):
                key_device = jnp.bitwise_xor(me, block // blocks_here)
                seen = mask_ref[t % blocks_here, key_device * blocks_here + block % blocks_here]
                tile = jnp.where(lane == block, jnp.where(seen == 1, 0.0, NEG), tile)
            mask_cols[t * BLOCK : (t + 1) * BLOCK, :] = tile.astype(low)
        for block in range(tiles):
            part = slice(block * BLOCK, (block + 1) * BLOCK)
            keys[part, HEAD_DIM:] = jnp.where(lane == block, 1.0, 0.0).astype(low)
            values[part, HEAD_DIM:] = jnp.where(lane < 3, 1.0, 0.0).astype(low)
        key_pos = lax.broadcasted_iota(jnp.int32, (BLOCK, BLOCK), 0)
        query_pos = lax.broadcasted_iota(jnp.int32, (BLOCK, BLOCK), 1)
        causal[...] = jnp.where(key_pos <= query_pos, 0.0, NEG)

    @pl.when(step == 0)
    def _():
        for piece in range(2 * pieces):
            part = slice(piece * half, (piece + 1) * half)
            column = piece % 2 * 2 * HEAD_DIM
            key_part = kv_refs[piece // 2][:, column : column + HEAD_DIM]
            value_part = kv_refs[piece // 2][:, column + HEAD_DIM : column + 2 * HEAD_DIM]
            keys[part, :HEAD_DIM] = key_part
            values[part, :HEAD_DIM] = value_part
            keys_t[:, part] = key_part.T
            values_t[:, part] = value_part.T
        key_acc[...] = jnp.zeros_like(key_acc)
        value_acc[...] = jnp.zeros_like(value_acc)

    state = [dict() for _ in range(per_step)]

    def take(own, peer, i):
        columns = slice(i * HEAD_DIM, (i + 1) * HEAD_DIM)
        return jnp.concatenate([own[0, :, columns], peer[0, :, columns]], axis=0)

    def fold(x, op):
        return op(x.reshape(x.shape[0] // 8, 8, x.shape[1]), axis=0)

    def score(i):
        query = jnp.concatenate([take(own_q, peer_q, i), mask_cols[...]], axis=1)
        top = None
        for tile in range(tiles):
            part = slice(tile * BLOCK, (tile + 1) * BLOCK)
            got = dot(keys[part, :], query, NT)
            if tile < blocks:
                here = slice(tile * BLOCK, (tile + 1) * BLOCK)
                cut = got[:, here] + causal[...]
                got = jnp.concatenate(
                    [x for x in (got[:, : here.start], cut, got[:, here.stop :]) if x.shape[1]], axis=1
                )
            scores[i, part, :] = got
            best = fold(got, jnp.max)
            top = best if top is None else jnp.maximum(top, best)
            yield
        state[i]["top"] = jnp.max(top, axis=0, keepdims=True) * exp_scale

    def soften(i):
        top = state[i]["top"]
        total = None
        for tile in range(tiles):
            part = slice(tile * BLOCK, (tile + 1) * BLOCK)
            weight = jnp.exp2(scores[i, part, :] * exp_scale - top)
            weights[part, i * rows : (i + 1) * rows] = weight.astype(low)
            add = fold(weight, jnp.sum)
            total = add if total is None else total + add
            yield
        state[i]["inverse"] = 1.0 / jnp.sum(total, axis=0, keepdims=True)

    def attend(i):
        columns = slice(i * HEAD_DIM, (i + 1) * HEAD_DIM)
        inverse = state[i]["inverse"]
        grad_t = (take(own_g, peer_g, i).T.astype(jnp.float32) * inverse).astype(low)
        out_t = None
        wide_tile = 2 * BLOCK
        for start in range(0, tiles * BLOCK, wide_tile):
            part = slice(start, start + wide_tile)
            got = dot(values_t[:, part], weights[part, i * rows : (i + 1) * rows])
            out_t = got if out_t is None else out_t + got
            yield
        out_t = out_t * inverse
        delta = -jnp.sum(out_t * grad_t.astype(jnp.float32), axis=0, keepdims=True)
        out = out_t.astype(low).T
        own_o[:, columns] = out[:half]
        peer_out[:, columns] = out[half:]
        first = delta.astype(low).astype(jnp.float32)
        second = (delta - first).astype(low).astype(jnp.float32)
        third = delta - first - second
        line = lax.broadcasted_iota(jnp.int32, (HEAD_DIM, rows), 0)
        extra = jnp.where(
            line == 0, first, jnp.where(line == 1, second, jnp.where(line == 2, third, 0.0))
        ).astype(low)
        state[i]["grad_t"] = grad_t
        state[i]["both_t"] = jnp.concatenate([grad_t, extra], axis=0)
        yield

    def flow(i):
        both_t = state[i]["both_t"]
        span = slice(i * rows, (i + 1) * rows)
        for tile in range(tiles):
            part = slice(tile * BLOCK, (tile + 1) * BLOCK)
            got = dot(values[part, :], both_t)
            flows[part, span] = (weights[part, span].astype(jnp.float32) * got).astype(low)
            yield

    def finish(i):
        columns = slice(i * HEAD_DIM, (i + 1) * HEAD_DIM)
        span = slice(i * rows, (i + 1) * rows)
        query_grad = (dot(keys_t[...], flows[:, span]) * score_scale).astype(low).T
        own_dq[:, columns] = query_grad[:half]
        start = (RATIO + i) * HEAD_DIM
        peer_out[:, start : start + HEAD_DIM] = query_grad[half:]
        yield

    def gather(i):
        if i % 2:
            span = slice((i - 1) * rows, (i + 1) * rows)
            grads_t = jnp.concatenate([state[j]["grad_t"] for j in (i - 1, i)], axis=1)
            queries = jnp.concatenate([take(own_q, peer_q, j) for j in (i - 1, i)], axis=0)
            for tile in range(tiles):
                part = slice(tile * BLOCK, (tile + 1) * BLOCK)
                value_acc[part, :] += dot(weights[part, span], grads_t, NT)
                key_acc[part, :] += dot(flows[part, span], queries)
                yield

    stages = [score, soften, attend, flow, finish, gather]
    for slot in range(per_step + len(stages) - 1):
        active = [
            stage(slot - lag)
            for lag, stage in reversed(list(enumerate(stages)))
            if 0 <= slot - lag < per_step
        ]
        done = object()
        while active:
            active = [work for work in active if next(work, done) is not done]

    @pl.when(step == steps - 1)
    def _():
        for piece in range(2 * pieces):
            part = slice(piece * half, (piece + 1) * half)
            column = piece % 2 * 2 * HEAD_DIM
            out = grad_refs[piece // 2]
            out[:, column : column + HEAD_DIM] = (key_acc[part, :] * score_scale).astype(low)
            out[:, column + HEAD_DIM : column + 2 * HEAD_DIM] = value_acc[part, :].astype(low)
        if span:
            copy_columns(pieces, span, wide, where_ref[0] // 2, inputs_ref, grad_refs, 4 * HEAD_DIM)


def attention(me, core, own_mask, peer_mask, queries, peer_q, out_grad, peer_g, kv_pieces, group, inputs=None, span=()):
    tokens = queries.shape[1]
    blocks_here = tokens // BLOCK
    rows = 2 * tokens
    pieces = len(kv_pieces)
    per_step = RATIO
    steps = RATIO // per_step
    wide = per_step * HEAD_DIM
    where = jnp.stack([me, core]).astype(jnp.int32)

    def heads_in(g, h, where_ref, *_):
        return (0, 0, (where_ref[1] * (KV_HEADS // 2) + group) * steps + h)

    def fixed(g, h, *_):
        return (0, 0)

    wide_in = inputs.shape[2] // (lax.axis_size("dp") * pieces) if span else 0
    extra = [inputs] if span else []
    grad_cols = 4 * HEAD_DIM + wide_in * len(span)
    keys_all = pieces * rows
    out_cols = RATIO * HEAD_DIM
    result = pl.pallas_call(
        functools.partial(attention_kernel, pieces, blocks_here, steps, per_step, span, wide_in),
        grid_spec=pltpu.PrefetchScalarGridSpec(
            num_scalar_prefetch=3,
            grid=(1, steps),
            in_specs=[pl.BlockSpec(x.shape, lambda *_: (0, 0, 0)) for x in extra]
            + [pl.BlockSpec((1, tokens, wide), heads_in)] * 4
            + [pl.BlockSpec((tokens, 4 * HEAD_DIM), fixed)] * pieces,
            out_specs=[pl.BlockSpec((tokens, wide), fixed)] * 2
            + [pl.BlockSpec((tokens, 2 * wide), fixed)]
            + [pl.BlockSpec((tokens, grad_cols), fixed)] * pieces,
            scratch_shapes=[
                pltpu.VMEM((rows, HEAD_DIM), jnp.bfloat16),
                pltpu.VMEM((BLOCK, BLOCK), jnp.float32),
                pltpu.VMEM((keys_all, 2 * HEAD_DIM), jnp.bfloat16),
                pltpu.VMEM((keys_all, 2 * HEAD_DIM), jnp.bfloat16),
                pltpu.VMEM((HEAD_DIM, keys_all), jnp.bfloat16),
                pltpu.VMEM((HEAD_DIM, keys_all), jnp.bfloat16),
                pltpu.VMEM((keys_all, HEAD_DIM), jnp.float32),
                pltpu.VMEM((keys_all, HEAD_DIM), jnp.float32),
                pltpu.VMEM((per_step, keys_all, rows), jnp.float32),
                pltpu.VMEM((keys_all, per_step * rows), jnp.bfloat16),
                pltpu.VMEM((keys_all, per_step * rows), jnp.bfloat16),
            ],
        ),
        out_shape=[jax.ShapeDtypeStruct((tokens, out_cols), jnp.bfloat16)] * 2
        + [jax.ShapeDtypeStruct((tokens, 2 * out_cols), jnp.bfloat16)]
        + [jax.ShapeDtypeStruct((tokens, grad_cols), jnp.bfloat16)] * pieces,
        compiler_params=pltpu.CompilerParams(vmem_limit_bytes=(16 << 20) + 8 * per_step * rows * keys_all + 2 * per_step * rows * keys_all),
        cost_estimate=pl.CostEstimate(
            flops=(24 if span else 1) * RATIO * rows * keys_all * HEAD_DIM,
            transcendentals=RATIO * rows * keys_all,
            bytes_accessed=16 * tokens * out_cols,
        ),
        name="attention",
    )(where, own_mask, peer_mask, *extra, queries, peer_q, out_grad, peer_g, *kv_pieces)
    return list(result[:3]), list(result[3:])


def small_call(kernel, name, scalars, operands, out_shape, cost=2_000_000, scratch=(), streamed=False):
    whole = pl.BlockSpec(memory_space=pltpu.VMEM)
    return pl.pallas_call(
        kernel,
        grid=(1,) if streamed else (),
        in_specs=[pl.BlockSpec(memory_space=pltpu.SMEM)]
        + [pl.BlockSpec(x.shape, lambda i, n=x.ndim: (0,) * n) if streamed else whole for x in operands],
        out_specs=jax.tree.map(lambda _: whole, out_shape),
        out_shape=out_shape,
        scratch_shapes=scratch,
        compiler_params=pltpu.CompilerParams(vmem_limit_bytes=32 * 1024 * 1024),
        cost_estimate=pl.CostEstimate(flops=0, transcendentals=0, bytes_accessed=cost),
        name=name,
    )(scalars, *operands)


def pick_kernel(scalar_ref, own, peer, *outs):
    for i, out in enumerate(outs):
        for j in range(4):
            source = (own, peer)[j // 2]
            start = (j % 2 * KV_HEADS + 2 * scalar_ref[0] + i) * HEAD_DIM
            lanes = pl.ds(pl.multiple_of(start, HEAD_DIM), HEAD_DIM)
            out[:, j * HEAD_DIM : (j + 1) * HEAD_DIM] = source[:, lanes]


def turn_kernel(offset, scalar_ref, *refs):
    *parts, out = refs
    tokens = parts[0].shape[0]
    for i, part in enumerate(parts):
        out[:, i * tokens : (i + 1) * tokens] = part[:, offset:].T


def product_kernel(plan, scale, scalar_ref, own_low, own_high, peer_low, peer_high, *refs):
    *refs, whole = refs
    pieces = len(refs) - len(plan)
    grads, outs = refs[:pieces], refs[pieces:]
    own_grad = jnp.concatenate([g[:, : 2 * HEAD_DIM] for g in grads], axis=0)
    peer_grad = jnp.concatenate([g[:, 2 * HEAD_DIM :] for g in grads], axis=0)
    half = own_low.shape[0]
    for i, (own, peer) in enumerate(((own_low, peer_low), (own_high, peer_high))):
        got = dot(own[...], own_grad) + dot(peer[...], peer_grad)
        whole[i * half : i * half + own.shape[0], :] = got * scale
    for chunks, out in zip(plan, outs):
        size = out.shape[0] // len(chunks)
        for i, k in enumerate(chunks):
            start = pl.multiple_of(jnp.bitwise_xor(scalar_ref[0], k) * size, size)
            out[i * size : (i + 1) * size, :] = whole[pl.ds(start, size), :].astype(out.dtype)


def pack_kernel(span, scalar_ref, inputs_ref, front, *outs):
    wide = (outs[0].shape[1] - front.shape[1]) // len(span)
    copy_columns(len(outs), span, wide, scalar_ref[0], inputs_ref, outs, front.shape[1])
    for out in outs[1:]:
        out[:, : front.shape[1]] = front[...]


def columns_for(inputs, me, k, chips, span):
    tokens, width = inputs.shape[1:]
    wide = width // (lax.axis_size("dp") * chips)
    shaped = inputs[0].reshape(tokens, -1, chips, wide)[:, span[0] : span[-1] + 1]
    part = lax.dynamic_index_in_dim(shaped, (me // 2) ^ k, 2, keepdims=False)
    return part.reshape(tokens, wide * len(span))


def pack(inputs, front, me, chips, span):
    tokens = inputs.shape[1]
    wide = inputs.shape[2] // (lax.axis_size("dp") * chips)
    if wide % HEAD_DIM:
        return [
            jnp.concatenate([front, columns_for(inputs, me, k, chips, span)], axis=1)
            for k in range(chips)
        ]
    return small_call(
        functools.partial(pack_kernel, span),
        "pack",
        (me // 2).reshape(1).astype(jnp.int32),
        [inputs, front],
        [jax.ShapeDtypeStruct((tokens, front.shape[1] + wide * len(span)), jnp.bfloat16)] * chips,
        cost=1,
    )


def settle_kernel(starts, scalar_ref, *refs):
    *parts, keep, send = refs
    size = keep.shape[0]
    core = scalar_ref[0]
    count = len(parts) // 2
    for first, out in ((core * size, keep), ((1 - core) * size, send)):
        for j in range(2):
            total = None
            for ref, start in zip(parts[j * count : (j + 1) * count], starts[j]):
                part = ref[pl.ds(pl.multiple_of(first + start, size), size), :].astype(jnp.float32)
                total = part if total is None else total + part
            out[:, j * 2 * HEAD_DIM : (j + 1) * 2 * HEAD_DIM] = total


def close_kernel(scalar_ref, keep, got, key_out, value_out):
    core = scalar_ref[0]
    for side, ref in ((core, keep), (1 - core, got)):
        for i in range(2):
            span = pl.ds(pl.multiple_of((2 * side + i) * HEAD_DIM, HEAD_DIM), HEAD_DIM)
            key_out[:, span] = ref[:, 2 * i * HEAD_DIM : (2 * i + 1) * HEAD_DIM]
            value_out[:, span] = ref[:, (2 * i + 1) * HEAD_DIM : (2 * i + 2) * HEAD_DIM]


def join_kernel(scalar_ref, own_o_a, own_o_b, own_dq_a, own_dq_b, got_a, got_b, out, query_grad, sem):
    core = scalar_ref[0]
    wide = own_o_a.shape[1]
    copies = []
    for j, (whole, own) in enumerate(((out, (own_o_a, own_o_b)), (query_grad, (own_dq_a, own_dq_b)))):
        for i in range(2):
            other = (got_a, got_b)[i].at[:, j * wide : (j + 1) * wide]
            for side, ref in ((core, own[i]), (1 - core, other)):
                span = pl.ds(pl.multiple_of((2 * side + i) * wide, wide), wide)
                copies.append(pltpu.make_async_copy(ref, whole.at[0, :, span], sem.at[len(copies)]))
    for copy in copies:
        copy.start()
    for copy in copies:
        copy.wait()


def join(core_scalar, parts, shape):
    return pl.pallas_call(
        join_kernel,
        in_specs=[pl.BlockSpec(memory_space=pltpu.SMEM)]
        + [pl.BlockSpec(memory_space=pl.ANY)] * len(parts),
        out_specs=[pl.BlockSpec(memory_space=pltpu.VMEM)] * 2,
        out_shape=[jax.ShapeDtypeStruct(shape, jnp.bfloat16)] * 2,
        scratch_shapes=[pltpu.SemaphoreType.DMA((8,))],
        cost_estimate=pl.CostEstimate(flops=0, transcendentals=0, bytes_accessed=4_000_000),
        name="join",
    )(core_scalar, *parts)


def hold(values, *others):
    return lax.optimization_barrier((values, others))[0]


def body(inputs, queries, keys_values, out_grad, tree_mask):
    tokens = queries.shape[1]
    width = queries.shape[2]
    count = lax.axis_size("ctx")
    data_size = lax.axis_size("dp")
    me = lax.axis_index("ctx")
    data_me = lax.axis_index("dp")
    core = me % 2
    chips = count // 2
    hops = [2 * p for p in range(1, chips)]
    low, high = jnp.bfloat16, jnp.float32
    core_scalar = core.reshape(1).astype(jnp.int32)
    data_scalar = data_me.reshape(1).astype(jnp.int32)

    flat = lax.optimization_barrier(keys_values.reshape(tokens, 2 * KV_HEADS * HEAD_DIM))
    own_a, own_b = small_call(
        pick_kernel,
        "pick",
        core_scalar,
        [flat, swap(flat, "ctx", 1)],
        [jax.ShapeDtypeStruct((tokens, 4 * HEAD_DIM), low)] * 2,
        cost=1,
    )
    pieces_a = [own_a] + [swap(own_a, "ctx", k) for k in hops]
    own_mask, queries_later, out_grad_later = hold((tree_mask[0], queries, out_grad), own_a)
    peer_mask = swap(own_mask, "ctx", 1)
    peer_q = swap(queries_later, "ctx", 1)
    peer_g = swap(out_grad_later, "ctx", 1)
    middle = data_size // 2
    whole_lanes = width // (data_size * chips) % HEAD_DIM == 0
    low_span, high_span = range(middle), range(middle, data_size)
    packed_b = pack(inputs, hold(own_b, peer_mask), me, chips, low_span)
    sends = hold(packed_b[1:], peer_q, peer_g)
    pieces_b = [own_b] + [swap(x, "ctx", k) for x, k in zip(sends, hops)]

    heads = (me, core, own_mask, peer_mask, queries, peer_q, out_grad, peer_g)
    if whole_lanes:
        outs_a, packed_a = attention(*heads, pieces_a, 0, inputs, high_span)
    else:
        outs_a, packed_a = attention(*heads, pieces_a, 0)
        packed_a = [
            jnp.concatenate([x, columns_for(inputs, me, k, chips, high_span)], axis=1)
            for k, x in enumerate(packed_a)
        ]
    back_a = [swap(x, "ctx", k) for x, k in zip(packed_a[1:], hops)]
    got_a = swap(outs_a[2], "ctx", 1)
    pieces_b = hold(pieces_b, outs_a[2])

    def turn(parts, streamed):
        return small_call(
            functools.partial(turn_kernel, 4 * HEAD_DIM),
            "turn",
            core_scalar,
            parts,
            jax.ShapeDtypeStruct((parts[0].shape[1] - 4 * HEAD_DIM, chips * tokens), low),
            cost=1,
            streamed=streamed,
        )

    own_low = turn(list(packed_b[:1]) + list(pieces_b[1:]), True)
    peer_low = swap(own_low, "ctx", 1)
    outs_b, grads_b = attention(*heads, pieces_b, 1)
    grads_b, back_a, got_a, peer_low = lax.optimization_barrier((grads_b, back_a, got_a, peer_low))
    back_b = [swap(x, "ctx", k) for x, k in zip(grads_b[1:], hops)]
    own_high = turn(list(packed_a[:1]) + list(back_a), False)
    peer_high = swap(own_high, "ctx", 1)

    def owned(mine, back):
        total = mine.astype(high)
        for x in back:
            total = total + x.astype(high)
        return total.astype(low)

    def gathered(total):
        return [total] + [swap(total, "ctx", k) for k in hops]

    scale = 1.0 / math.sqrt(tokens * count * data_size)
    rows_out = width // (data_size * count)
    size = 2 * rows_out
    pairwise = data_size == 4
    plan = [[0], [2], [3, 1]] if pairwise else [[k] for k in range(data_size)]
    kinds = [high, high, low] if pairwise else [high] + [low] * (data_size - 1)

    def product(grads, plan, kinds):
        return small_call(
            functools.partial(product_kernel, plan, scale),
            "product",
            data_scalar,
            [own_low, own_high, peer_low, peer_high] + grads,
            [
                jax.ShapeDtypeStruct((size * len(chunks), 2 * HEAD_DIM), kind)
                for chunks, kind in zip(plan, kinds)
            ],
            scratch=[pltpu.VMEM((size * data_size, 2 * HEAD_DIM), high)],
        )

    folded = 4 * HEAD_DIM
    all_a = gathered(owned(packed_a[0][:, :folded], [x[:, :folded] for x in back_a]))
    all_b = gathered(owned(grads_b[0], back_b))
    chunks_a = product(all_a, plan, kinds)
    all_b = hold(all_b, chunks_a)
    if pairwise:
        plan, kinds = [[0], [2], [3], [1]], [high, high, low, low]
    chunks_b = product(all_b, plan, kinds)
    if pairwise:
        near_a = swap(chunks_a[2], "dp", 1)
        cross_a = (chunks_a[1] + near_a[:size].astype(high)).astype(low)
        far_a = swap(cross_a, "dp", 2)
        near_b = swap(hold(chunks_b[2], far_a), "dp", 1)
        cross_b = (chunks_b[1] + near_b.astype(high)).astype(low)
        far_b = swap(cross_b, "dp", 2)
        beside = swap(hold(chunks_b[3], cross_b), "dp", 1)
        arrived = [[near_a, far_a], [beside, far_b]]
        starts = [[0, size, 0], [0, 0, 0]]
    else:
        arrived = [[swap(x[k], "dp", k) for k in range(1, data_size)] for x in (chunks_a, chunks_b)]
        cross_b = chunks_b[0]
        starts = [[0] * data_size] * 2
    got_b = swap(hold(outs_b[2], chunks_a), "ctx", 1)
    parts = [outs_a[0], outs_b[0], outs_a[1], outs_b[1], got_a, got_b]
    attn_out, query_grad = join(core_scalar, hold(parts, arrived[0], chunks_b), queries.shape)
    arrived, attn_out, query_grad = lax.optimization_barrier((arrived, attn_out, query_grad))
    kept, sent = small_call(
        functools.partial(settle_kernel, starts),
        "settle",
        core_scalar,
        [chunks_a[0]] + arrived[0] + [chunks_b[0]] + arrived[1],
        [jax.ShapeDtypeStruct((rows_out, 4 * HEAD_DIM), high)] * 2,
    )
    key_out, value_out = small_call(
        close_kernel,
        "close",
        core_scalar,
        [kept, swap(sent, "ctx", 1)],
        [jax.ShapeDtypeStruct((rows_out, KV_HEADS * HEAD_DIM), high)] * 2,
    )
    return attn_out, query_grad, key_out, value_out


def solution(mesh):
    in_specs = (
        P("dp", "ctx", None),
        P("dp", "ctx", None),
        P("dp", "ctx", None, None),
        P("dp", "ctx", None),
        P("dp", "ctx", None),
    )
    out_specs = (
        P("dp", "ctx", None),
        P("dp", "ctx", None),
        P(("dp", "ctx"), None),
        P(("dp", "ctx"), None),
    )
    return jax.shard_map(body, mesh=mesh, in_specs=in_specs, out_specs=out_specs, check_vma=False)
```

```python
import functools
import math

import jax
import jax.numpy as jnp
from jax import lax
from jax.experimental import pallas as pl
from jax.experimental.pallas import tpu as pltpu
from jax.sharding import PartitionSpec as P

HEADS = 32
KV_HEADS = 4
HEAD_DIM = 128
BLOCK = 128
RATIO = HEADS // KV_HEADS
NEG = -1e30
NT = (((1,), (1,)), ((), ()))


def swap(value, axis, mask):
    pairs = [(i, i ^ mask) for i in range(lax.axis_size(axis))]
    return lax.ppermute(value, axis, pairs)


def dot(a, b, dims=(((1,), (0,)), ((), ()))):
    return lax.dot_general(a, b, dims, preferred_element_type=jnp.float32)


def copy_columns(chips, span, wide, chip, inputs_ref, outs, start):
    for k, out in enumerate(outs):
        for i, d in enumerate(span):
            source = pl.ds(pl.multiple_of((d * chips + jnp.bitwise_xor(chip, k)) * wide, wide), wide)
            out[:, start + i * wide : start + (i + 1) * wide] = inputs_ref[0, :, source]


def attention_kernel(pieces, blocks_here, steps, per_step, span, wide, where_ref, own_mask, peer_mask, *refs):
    if span:
        inputs_ref, *refs = refs
    own_q, peer_q, own_g, peer_g = refs[:4]
    kv_refs = refs[4 : 4 + pieces]
    own_o, own_dq, peer_out = refs[4 + pieces : 7 + pieces]
    grad_refs = refs[7 + pieces : 7 + 2 * pieces]
    (mask_cols, causal, keys, values, keys_t, values_t, key_acc, value_acc, scores, weights, flows) = refs[
        7 + 2 * pieces :
    ]
    group, step = pl.program_id(0), pl.program_id(1)
    rows = 2 * blocks_here * BLOCK
    half = rows // 2
    blocks = 2 * blocks_here
    tiles = pieces * blocks
    score_scale = 1.0 / math.sqrt(HEAD_DIM)
    exp_scale = score_scale * math.log2(math.e)
    low = jnp.bfloat16

    @pl.when((group == 0) & (step == 0))
    def _():
        me = where_ref[0]
        lane = lax.broadcasted_iota(jnp.int32, (BLOCK, HEAD_DIM), 1)
        for t in range(blocks):
            mask_ref = own_mask if t < blocks_here else peer_mask
            tile = jnp.zeros((BLOCK, HEAD_DIM), jnp.float32)
            for block in range(tiles):
                key_device = jnp.bitwise_xor(me, block // blocks_here)
                seen = mask_ref[t % blocks_here, key_device * blocks_here + block % blocks_here]
                tile = jnp.where(lane == block, jnp.where(seen == 1, 0.0, NEG), tile)
            mask_cols[t * BLOCK : (t + 1) * BLOCK, :] = tile.astype(low)
        for block in range(tiles):
            part = slice(block * BLOCK, (block + 1) * BLOCK)
            keys[part, HEAD_DIM:] = jnp.where(lane == block, 1.0, 0.0).astype(low)
            values[part, HEAD_DIM:] = jnp.where(lane < 3, 1.0, 0.0).astype(low)
        key_pos = lax.broadcasted_iota(jnp.int32, (BLOCK, BLOCK), 0)
        query_pos = lax.broadcasted_iota(jnp.int32, (BLOCK, BLOCK), 1)
        causal[...] = jnp.where(key_pos <= query_pos, 0.0, NEG)

    @pl.when(step == 0)
    def _():
        for piece in range(2 * pieces):
            part = slice(piece * half, (piece + 1) * half)
            column = piece % 2 * 2 * HEAD_DIM
            key_part = kv_refs[piece // 2][:, column : column + HEAD_DIM]
            value_part = kv_refs[piece // 2][:, column + HEAD_DIM : column + 2 * HEAD_DIM]
            keys[part, :HEAD_DIM] = key_part
            values[part, :HEAD_DIM] = value_part
            keys_t[:, part] = key_part.T
            values_t[:, part] = value_part.T
        key_acc[...] = jnp.zeros_like(key_acc)
        value_acc[...] = jnp.zeros_like(value_acc)

    state = [dict() for _ in range(per_step)]

    def take(own, peer, i):
        columns = slice(i * HEAD_DIM, (i + 1) * HEAD_DIM)
        return jnp.concatenate([own[0, :, columns], peer[0, :, columns]], axis=0)

    def fold(x, op):
        return op(x.reshape(x.shape[0] // 8, 8, x.shape[1]), axis=0)

    def score(i):
        query = jnp.concatenate([take(own_q, peer_q, i), mask_cols[...]], axis=1)
        top = None
        for tile in range(tiles):
            part = slice(tile * BLOCK, (tile + 1) * BLOCK)
            got = dot(keys[part, :], query, NT)
            if tile < blocks:
                here = slice(tile * BLOCK, (tile + 1) * BLOCK)
                cut = got[:, here] + causal[...]
                got = jnp.concatenate(
                    [x for x in (got[:, : here.start], cut, got[:, here.stop :]) if x.shape[1]], axis=1
                )
            scores[i, part, :] = got
            best = fold(got, jnp.max)
            top = best if top is None else jnp.maximum(top, best)
            yield
        state[i]["top"] = jnp.max(top, axis=0, keepdims=True) * exp_scale

    def soften(i):
        top = state[i]["top"]
        total = None
        for tile in range(tiles):
            part = slice(tile * BLOCK, (tile + 1) * BLOCK)
            weight = jnp.exp2(scores[i, part, :] * exp_scale - top)
            weights[part, i * rows : (i + 1) * rows] = weight.astype(low)
            add = fold(weight, jnp.sum)
            total = add if total is None else total + add
            yield
        state[i]["inverse"] = 1.0 / jnp.sum(total, axis=0, keepdims=True)

    def attend(i):
        columns = slice(i * HEAD_DIM, (i + 1) * HEAD_DIM)
        inverse = state[i]["inverse"]
        grad_t = (take(own_g, peer_g, i).T.astype(jnp.float32) * inverse).astype(low)
        out_t = None
        wide_tile = 2 * BLOCK
        for start in range(0, tiles * BLOCK, wide_tile):
            part = slice(start, start + wide_tile)
            got = dot(values_t[:, part], weights[part, i * rows : (i + 1) * rows])
            out_t = got if out_t is None else out_t + got
            yield
        out_t = out_t * inverse
        delta = -jnp.sum(out_t * grad_t.astype(jnp.float32), axis=0, keepdims=True)
        out = out_t.astype(low).T
        own_o[:, columns] = out[:half]
        peer_out[:, columns] = out[half:]
        first = delta.astype(low).astype(jnp.float32)
        second = (delta - first).astype(low).astype(jnp.float32)
        third = delta - first - second
        line = lax.broadcasted_iota(jnp.int32, (HEAD_DIM, rows), 0)
        extra = jnp.where(
            line == 0, first, jnp.where(line == 1, second, jnp.where(line == 2, third, 0.0))
        ).astype(low)
        state[i]["grad_t"] = grad_t
        state[i]["both_t"] = jnp.concatenate([grad_t, extra], axis=0)
        yield

    def flow(i):
        both_t = state[i]["both_t"]
        span = slice(i * rows, (i + 1) * rows)
        for tile in range(tiles):
            part = slice(tile * BLOCK, (tile + 1) * BLOCK)
            got = dot(values[part, :], both_t)
            flows[part, span] = (weights[part, span].astype(jnp.float32) * got).astype(low)
            yield

    def finish(i):
        columns = slice(i * HEAD_DIM, (i + 1) * HEAD_DIM)
        span = slice(i * rows, (i + 1) * rows)
        query_grad = (dot(keys_t[...], flows[:, span]) * score_scale).astype(low).T
        own_dq[:, columns] = query_grad[:half]
        start = (RATIO + i) * HEAD_DIM
        peer_out[:, start : start + HEAD_DIM] = query_grad[half:]
        yield

    def gather(i):
        if i % 2:
            span = slice((i - 1) * rows, (i + 1) * rows)
            grads_t = jnp.concatenate([state[j]["grad_t"] for j in (i - 1, i)], axis=1)
            queries = jnp.concatenate([take(own_q, peer_q, j) for j in (i - 1, i)], axis=0)
            for tile in range(tiles):
                part = slice(tile * BLOCK, (tile + 1) * BLOCK)
                value_acc[part, :] += dot(weights[part, span], grads_t, NT)
                key_acc[part, :] += dot(flows[part, span], queries)
                yield

    stages = [score, soften, attend, flow, finish, gather]
    for slot in range(per_step + len(stages) - 1):
        active = [
            stage(slot - lag)
            for lag, stage in reversed(list(enumerate(stages)))
            if 0 <= slot - lag < per_step
        ]
        done = object()
        while active:
            active = [work for work in active if next(work, done) is not done]

    @pl.when(step == steps - 1)
    def _():
        for piece in range(2 * pieces):
            part = slice(piece * half, (piece + 1) * half)
            column = piece % 2 * 2 * HEAD_DIM
            out = grad_refs[piece // 2]
            out[:, column : column + HEAD_DIM] = (key_acc[part, :] * score_scale).astype(low)
            out[:, column + HEAD_DIM : column + 2 * HEAD_DIM] = value_acc[part, :].astype(low)
        if span:
            copy_columns(pieces, span, wide, where_ref[0] // 2, inputs_ref, grad_refs, 4 * HEAD_DIM)


def attention(me, core, own_mask, peer_mask, queries, peer_q, out_grad, peer_g, kv_pieces, group, inputs=None, span=()):
    tokens = queries.shape[1]
    blocks_here = tokens // BLOCK
    rows = 2 * tokens
    pieces = len(kv_pieces)
    per_step = RATIO
    steps = RATIO // per_step
    wide = per_step * HEAD_DIM
    where = jnp.stack([me, core]).astype(jnp.int32)

    def heads_in(g, h, where_ref, *_):
        return (0, 0, (where_ref[1] * (KV_HEADS // 2) + group) * steps + h)

    def fixed(g, h, *_):
        return (0, 0)

    wide_in = inputs.shape[2] // (lax.axis_size("dp") * pieces) if span else 0
    extra = [inputs] if span else []
    grad_cols = 4 * HEAD_DIM + wide_in * len(span)
    keys_all = pieces * rows
    out_cols = RATIO * HEAD_DIM
    result = pl.pallas_call(
        functools.partial(attention_kernel, pieces, blocks_here, steps, per_step, span, wide_in),
        grid_spec=pltpu.PrefetchScalarGridSpec(
            num_scalar_prefetch=3,
            grid=(1, steps),
            in_specs=[pl.BlockSpec(x.shape, lambda *_: (0, 0, 0)) for x in extra]
            + [pl.BlockSpec((1, tokens, wide), heads_in)] * 4
            + [pl.BlockSpec((tokens, 4 * HEAD_DIM), fixed)] * pieces,
            out_specs=[pl.BlockSpec((tokens, wide), fixed)] * 2
            + [pl.BlockSpec((tokens, 2 * wide), fixed)]
            + [pl.BlockSpec((tokens, grad_cols), fixed)] * pieces,
            scratch_shapes=[
                pltpu.VMEM((rows, HEAD_DIM), jnp.bfloat16),
                pltpu.VMEM((BLOCK, BLOCK), jnp.float32),
                pltpu.VMEM((keys_all, 2 * HEAD_DIM), jnp.bfloat16),
                pltpu.VMEM((keys_all, 2 * HEAD_DIM), jnp.bfloat16),
                pltpu.VMEM((HEAD_DIM, keys_all), jnp.bfloat16),
                pltpu.VMEM((HEAD_DIM, keys_all), jnp.bfloat16),
                pltpu.VMEM((keys_all, HEAD_DIM), jnp.float32),
                pltpu.VMEM((keys_all, HEAD_DIM), jnp.float32),
                pltpu.VMEM((per_step, keys_all, rows), jnp.float32),
                pltpu.VMEM((keys_all, per_step * rows), jnp.bfloat16),
                pltpu.VMEM((keys_all, per_step * rows), jnp.bfloat16),
            ],
        ),
        out_shape=[jax.ShapeDtypeStruct((tokens, out_cols), jnp.bfloat16)] * 2
        + [jax.ShapeDtypeStruct((tokens, 2 * out_cols), jnp.bfloat16)]
        + [jax.ShapeDtypeStruct((tokens, grad_cols), jnp.bfloat16)] * pieces,
        compiler_params=pltpu.CompilerParams(vmem_limit_bytes=(16 << 20) + 8 * per_step * rows * keys_all + 2 * per_step * rows * keys_all),
        cost_estimate=pl.CostEstimate(
            flops=(24 if span else 1) * RATIO * rows * keys_all * HEAD_DIM,
            transcendentals=RATIO * rows * keys_all,
            bytes_accessed=16 * tokens * out_cols,
        ),
        name="attention",
    )(where, own_mask, peer_mask, *extra, queries, peer_q, out_grad, peer_g, *kv_pieces)
    return list(result[:3]), list(result[3:])


def small_call(kernel, name, scalars, operands, out_shape, cost=2_000_000, scratch=(), streamed=False):
    whole = pl.BlockSpec(memory_space=pltpu.VMEM)
    return pl.pallas_call(
        kernel,
        grid=(1,) if streamed else (),
        in_specs=[pl.BlockSpec(memory_space=pltpu.SMEM)]
        + [pl.BlockSpec(x.shape, lambda i, n=x.ndim: (0,) * n) if streamed else whole for x in operands],
        out_specs=jax.tree.map(lambda _: whole, out_shape),
        out_shape=out_shape,
        scratch_shapes=scratch,
        compiler_params=pltpu.CompilerParams(vmem_limit_bytes=32 * 1024 * 1024),
        cost_estimate=pl.CostEstimate(flops=0, transcendentals=0, bytes_accessed=cost),
        name=name,
    )(scalars, *operands)


def pick_kernel(scalar_ref, own, peer, *outs):
    for i, out in enumerate(outs):
        for j in range(4):
            source = (own, peer)[j // 2]
            start = (j % 2 * KV_HEADS + 2 * scalar_ref[0] + i) * HEAD_DIM
            lanes = pl.ds(pl.multiple_of(start, HEAD_DIM), HEAD_DIM)
            out[:, j * HEAD_DIM : (j + 1) * HEAD_DIM] = source[:, lanes]


def turn_kernel(offset, scalar_ref, *refs):
    *parts, out = refs
    tokens = parts[0].shape[0]
    for i, part in enumerate(parts):
        out[:, i * tokens : (i + 1) * tokens] = part[:, offset:].T


def product_kernel(plan, scale, scalar_ref, own_low, own_high, peer_low, peer_high, *refs):
    *refs, whole = refs
    pieces = len(refs) - len(plan)
    grads, outs = refs[:pieces], refs[pieces:]
    own_grad = jnp.concatenate([g[:, : 2 * HEAD_DIM] for g in grads], axis=0)
    peer_grad = jnp.concatenate([g[:, 2 * HEAD_DIM :] for g in grads], axis=0)
    half = own_low.shape[0]
    for i, (own, peer) in enumerate(((own_low, peer_low), (own_high, peer_high))):
        got = dot(own[...], own_grad) + dot(peer[...], peer_grad)
        whole[i * half : i * half + own.shape[0], :] = got * scale
    for chunks, out in zip(plan, outs):
        size = out.shape[0] // len(chunks)
        for i, k in enumerate(chunks):
            start = pl.multiple_of(jnp.bitwise_xor(scalar_ref[0], k) * size, size)
            out[i * size : (i + 1) * size, :] = whole[pl.ds(start, size), :].astype(out.dtype)


def pack_kernel(span, scalar_ref, inputs_ref, front, *outs):
    wide = (outs[0].shape[1] - front.shape[1]) // len(span)
    copy_columns(len(outs), span, wide, scalar_ref[0], inputs_ref, outs, front.shape[1])
    for out in outs[1:]:
        out[:, : front.shape[1]] = front[...]


def columns_for(inputs, me, k, chips, span):
    tokens, width = inputs.shape[1:]
    wide = width // (lax.axis_size("dp") * chips)
    shaped = inputs[0].reshape(tokens, -1, chips, wide)[:, span[0] : span[-1] + 1]
    part = lax.dynamic_index_in_dim(shaped, (me // 2) ^ k, 2, keepdims=False)
    return part.reshape(tokens, wide * len(span))


def pack(inputs, front, me, chips, span):
    tokens = inputs.shape[1]
    wide = inputs.shape[2] // (lax.axis_size("dp") * chips)
    if wide % HEAD_DIM:
        return [
            jnp.concatenate([front, columns_for(inputs, me, k, chips, span)], axis=1)
            for k in range(chips)
        ]
    return small_call(
        functools.partial(pack_kernel, span),
        "pack",
        (me // 2).reshape(1).astype(jnp.int32),
        [inputs, front],
        [jax.ShapeDtypeStruct((tokens, front.shape[1] + wide * len(span)), jnp.bfloat16)] * chips,
        cost=1,
    )


def settle_kernel(starts, scalar_ref, *refs):
    *parts, keep, send = refs
    size = keep.shape[0]
    core = scalar_ref[0]
    count = len(parts) // 2
    for first, out in ((core * size, keep), ((1 - core) * size, send)):
        for j in range(2):
            total = None
            for ref, start in zip(parts[j * count : (j + 1) * count], starts[j]):
                part = ref[pl.ds(pl.multiple_of(first + start, size), size), :].astype(jnp.float32)
                total = part if total is None else total + part
            out[:, j * 2 * HEAD_DIM : (j + 1) * 2 * HEAD_DIM] = total


def close_kernel(scalar_ref, keep, got, key_out, value_out):
    core = scalar_ref[0]
    for side, ref in ((core, keep), (1 - core, got)):
        for i in range(2):
            span = pl.ds(pl.multiple_of((2 * side + i) * HEAD_DIM, HEAD_DIM), HEAD_DIM)
            key_out[:, span] = ref[:, 2 * i * HEAD_DIM : (2 * i + 1) * HEAD_DIM]
            value_out[:, span] = ref[:, (2 * i + 1) * HEAD_DIM : (2 * i + 2) * HEAD_DIM]


def join_kernel(scalar_ref, own_o_a, own_o_b, own_dq_a, own_dq_b, got_a, got_b, out, query_grad, sem):
    core = scalar_ref[0]
    wide = own_o_a.shape[1]
    copies = []
    for j, (whole, own) in enumerate(((out, (own_o_a, own_o_b)), (query_grad, (own_dq_a, own_dq_b)))):
        for i in range(2):
            other = (got_a, got_b)[i].at[:, j * wide : (j + 1) * wide]
            for side, ref in ((core, own[i]), (1 - core, other)):
                span = pl.ds(pl.multiple_of((2 * side + i) * wide, wide), wide)
                copies.append(pltpu.make_async_copy(ref, whole.at[0, :, span], sem.at[len(copies)]))
    for copy in copies:
        copy.start()
    for copy in copies:
        copy.wait()


def join(core_scalar, parts, shape):
    return pl.pallas_call(
        join_kernel,
        in_specs=[pl.BlockSpec(memory_space=pltpu.SMEM)]
        + [pl.BlockSpec(memory_space=pl.ANY)] * len(parts),
        out_specs=[pl.BlockSpec(memory_space=pltpu.VMEM)] * 2,
        out_shape=[jax.ShapeDtypeStruct(shape, jnp.bfloat16)] * 2,
        scratch_shapes=[pltpu.SemaphoreType.DMA((8,))],
        cost_estimate=pl.CostEstimate(flops=0, transcendentals=0, bytes_accessed=4_000_000),
        name="join",
    )(core_scalar, *parts)


def hold(values, *others):
    return lax.optimization_barrier((values, others))[0]


def body(inputs, queries, keys_values, out_grad, tree_mask):
    tokens = queries.shape[1]
    width = queries.shape[2]
    count = lax.axis_size("ctx")
    data_size = lax.axis_size("dp")
    me = lax.axis_index("ctx")
    data_me = lax.axis_index("dp")
    core = me % 2
    chips = count // 2
    hops = [2 * p for p in range(1, chips)]
    low, high = jnp.bfloat16, jnp.float32
    core_scalar = core.reshape(1).astype(jnp.int32)
    data_scalar = data_me.reshape(1).astype(jnp.int32)

    flat = lax.optimization_barrier(keys_values.reshape(tokens, 2 * KV_HEADS * HEAD_DIM))
    own_a, own_b = small_call(
        pick_kernel,
        "pick",
        core_scalar,
        [flat, swap(flat, "ctx", 1)],
        [jax.ShapeDtypeStruct((tokens, 4 * HEAD_DIM), low)] * 2,
        cost=1,
    )
    pieces_a = [own_a] + [swap(own_a, "ctx", k) for k in hops]
    own_mask, queries_later, out_grad_later = hold((tree_mask[0], queries, out_grad), own_a)
    peer_mask = swap(own_mask, "ctx", 1)
    peer_q = swap(queries_later, "ctx", 1)
    peer_g = swap(out_grad_later, "ctx", 1)
    middle = data_size // 2
    whole_lanes = width // (data_size * chips) % HEAD_DIM == 0
    low_span, high_span = range(middle), range(middle, data_size)
    packed_b = pack(inputs, hold(own_b, peer_mask), me, chips, low_span)
    sends = hold(packed_b[1:], peer_q, peer_g)
    pieces_b = [own_b] + [swap(x, "ctx", k) for x, k in zip(sends, hops)]

    heads = (me, core, own_mask, peer_mask, queries, peer_q, out_grad, peer_g)
    if whole_lanes:
        outs_a, packed_a = attention(*heads, pieces_a, 0, inputs, high_span)
    else:
        outs_a, packed_a = attention(*heads, pieces_a, 0)
        packed_a = [
            jnp.concatenate([x, columns_for(inputs, me, k, chips, high_span)], axis=1)
            for k, x in enumerate(packed_a)
        ]
    back_a = [swap(x, "ctx", k) for x, k in zip(packed_a[1:], hops)]
    pieces_b = hold(pieces_b, outs_a[2])

    def turn(parts, streamed):
        return small_call(
            functools.partial(turn_kernel, 4 * HEAD_DIM),
            "turn",
            core_scalar,
            parts,
            jax.ShapeDtypeStruct((parts[0].shape[1] - 4 * HEAD_DIM, chips * tokens), low),
            cost=1,
            streamed=streamed,
        )

    own_low = turn(list(packed_b[:1]) + list(pieces_b[1:]), True)
    peer_low = swap(own_low, "ctx", 1)
    outs_b, grads_b = attention(*heads, pieces_b, 1)
    grads_b, back_a, peer_low = lax.optimization_barrier((grads_b, back_a, peer_low))
    back_b = [swap(x, "ctx", k) for x, k in zip(grads_b[1:], hops)]
    own_high = turn(list(packed_a[:1]) + list(back_a), False)
    peer_high = swap(own_high, "ctx", 1)

    def owned(mine, back):
        total = mine.astype(high)
        for x in back:
            total = total + x.astype(high)
        return total.astype(low)

    def gathered(total):
        return [total] + [swap(total, "ctx", k) for k in hops]

    scale = 1.0 / math.sqrt(tokens * count * data_size)
    rows_out = width // (data_size * count)
    size = 2 * rows_out
    pairwise = data_size == 4
    plan = [[0], [2], [3, 1]] if pairwise else [[k] for k in range(data_size)]
    kinds = [high, high, low] if pairwise else [high] + [low] * (data_size - 1)

    def product(grads, plan, kinds):
        return small_call(
            functools.partial(product_kernel, plan, scale),
            "product",
            data_scalar,
            [own_low, own_high, peer_low, peer_high] + grads,
            [
                jax.ShapeDtypeStruct((size * len(chunks), 2 * HEAD_DIM), kind)
                for chunks, kind in zip(plan, kinds)
            ],
            scratch=[pltpu.VMEM((size * data_size, 2 * HEAD_DIM), high)],
        )

    folded = 4 * HEAD_DIM
    all_a = gathered(owned(packed_a[0][:, :folded], [x[:, :folded] for x in back_a]))
    all_b = gathered(owned(grads_b[0], back_b))
    chunks_a = product(all_a, plan, kinds)
    all_b = hold(all_b, chunks_a)
    if pairwise:
        plan, kinds = [[0], [2], [3], [1]], [high, high, low, low]
    chunks_b = product(all_b, plan, kinds)
    if pairwise:
        near_a = swap(chunks_a[2], "dp", 1)
        cross_a = (chunks_a[1] + near_a[:size].astype(high)).astype(low)
        far_a = swap(cross_a, "dp", 2)
        near_b = swap(hold(chunks_b[2], far_a), "dp", 1)
        cross_b = (chunks_b[1] + near_b.astype(high)).astype(low)
        far_b = swap(cross_b, "dp", 2)
        beside = swap(hold(chunks_b[3], cross_b), "dp", 1)
        arrived = [[near_a, far_a], [beside, far_b]]
        starts = [[0, size, 0], [0, 0, 0]]
    else:
        arrived = [[swap(x[k], "dp", k) for k in range(1, data_size)] for x in (chunks_a, chunks_b)]
        cross_b = chunks_b[0]
        starts = [[0] * data_size] * 2
    got_a = swap(hold(outs_a[2], chunks_b), "ctx", 1)
    got_b = swap(hold(outs_b[2], chunks_a), "ctx", 1)
    parts = [outs_a[0], outs_b[0], outs_a[1], outs_b[1], got_a, got_b]
    attn_out, query_grad = join(core_scalar, hold(parts, arrived[0], chunks_b), queries.shape)
    arrived, attn_out, query_grad = lax.optimization_barrier((arrived, attn_out, query_grad))
    kept, sent = small_call(
        functools.partial(settle_kernel, starts),
        "settle",
        core_scalar,
        [chunks_a[0]] + arrived[0] + [chunks_b[0]] + arrived[1],
        [jax.ShapeDtypeStruct((rows_out, 4 * HEAD_DIM), high)] * 2,
    )
    key_out, value_out = small_call(
        close_kernel,
        "close",
        core_scalar,
        [kept, swap(sent, "ctx", 1)],
        [jax.ShapeDtypeStruct((rows_out, KV_HEADS * HEAD_DIM), high)] * 2,
    )
    return attn_out, query_grad, key_out, value_out


def solution(mesh):
    in_specs = (
        P("dp", "ctx", None),
        P("dp", "ctx", None),
        P("dp", "ctx", None, None),
        P("dp", "ctx", None),
        P("dp", "ctx", None),
    )
    out_specs = (
        P("dp", "ctx", None),
        P("dp", "ctx", None),
        P(("dp", "ctx"), None),
        P(("dp", "ctx"), None),
    )
    return jax.shard_map(body, mesh=mesh, in_specs=in_specs, out_specs=out_specs, check_vma=False)
```
